32 devices in a mesh: win: 2 (over y), chan: 16 (over z, x, core), tm: 1.
Axes of the slice: x: 2, y: 2, z: 4, core: 2. Of those that a mesh axis runs over, the one named last changes fastest.
Arguments:
- records: float32 [1024, 32768], P(('win', 'chan'), 'tm'), parts along dimension 0, may hold values from -1000 to 1000
- dead_mask: int32 [1024], P(('win', 'chan')), parts along dimension 0, may hold values 0 or 1
- offsets: int32 [16], P('win'), parts along dimension 0, may hold values from 0 to 511, as said below
Outputs:
- correlations: bfloat16 [32, 1024, 256], P('tm', ('win', 'chan')), parts along dimension 1
The draws below stay inside these ranges and needn't reach their ends.
There are 2 independent parts, one for each index of `win`. The reference program is written for one: setup_inputs(seed, part) draws one part's arguments, and reference() takes and returns one part's arrays. A program takes and returns all parts, laid end to end along the dimension named above; each array names one. Nothing has to cross between parts.
Inputs may be any that keep to these rules, and one draw needn't show every extreme that they name: `dead_mask`: 1 marks a dead channel. Window w begins at sample w * 4096 + offsets[w]; some window has offset 512 - 1.
All inputs are finite; a program needn't handle non-finite values. No bound on the sum of `dead_mask` on one device may be relied on, other than what follows from the above.
Results may differ from the reference program's by a relative error of at most 0.0033.
Values may be sent and summed in bfloat16 or wider, within the bound.
A program may use at most 64 MiB of HBM per device.

```python
import math
import jax
import jax.numpy as jnp
from jax import lax

L = 8192
HOP = 4096
JIT = 512
H = 128
K0 = 32
NF = 256
WB = 64
NLAG = 32
NPART = 256
NCH = 512
NS = 32768
NWIN = 8


TWO_PI = 2.0 * math.pi


def draw_records(key, part):
    key_list = jax.random.split(jax.random.fold_in(key, 11), 6)
    chan_pos = jnp.arange(NCH, dtype=jnp.float32)[:, None]
    time_pos = jnp.arange(NS, dtype=jnp.float32)[None, :]
    noise_part = jnp.clip(jax.random.normal(key_list[0], (NCH, NS), jnp.float32), -6.0, 6.0)
    spread = 1.2
    channel_gains = jnp.exp(jax.random.uniform(key_list[1], (NCH, 1), jnp.float32, -2.3, 2.3))
    blocks_count = (NS + 31) // 32
    envelope = jnp.exp(jax.random.uniform(key_list[2], (1, blocks_count), jnp.float32, -spread, spread))
    envelope = jnp.repeat(envelope, 32, axis=1)[:, :NS]
    frequencies = jax.random.uniform(key_list[3], (3,), jnp.float32, K0 / L, (K0 + NF) / L)
    delays = jax.random.uniform(key_list[4], (3,), jnp.float32, 0.1, 0.5)
    phases = jax.random.uniform(key_list[5], (3,), jnp.float32, 0.0, 6.28)
    wave_field = jnp.zeros((NCH, NS), jnp.float32)
    for wave_index in range(3):
        wave_field = wave_field + jnp.sin(TWO_PI * frequencies[wave_index] * (time_pos - delays[wave_index] * chan_pos) + phases[wave_index])
    return (channel_gains * envelope * (noise_part + 0.7 * wave_field)).astype(jnp.float32)


def draw_offsets(key, part):
    first_key = jax.random.fold_in(key, 21)
    second_key = jax.random.fold_in(key, 22)
    values = jax.random.randint(first_key, (NWIN,), 0, JIT, dtype=jnp.int32)
    chosen = jax.random.randint(second_key, (), 0, NWIN, dtype=jnp.int32)
    return jnp.where(jnp.arange(NWIN, dtype=jnp.int32) == chosen, JIT - 1, values).astype(jnp.int32)


def touch_ends(values, stream_key, low, largest):
    spot = [jax.random.randint(jax.random.fold_in(stream_key, axis), (), 0, length) for axis, length in enumerate(values.shape)]
    longest = values.shape.index(max(values.shape))
    next_to = spot[:longest] + [(spot[longest] + 1) % values.shape[longest]] + spot[longest + 1:]
    return values.at[tuple(spot)].set(low).at[tuple(next_to)].set(largest)


def setup_inputs(seed: int = 0, part: int = 0) -> dict:
    seeds = jax.random.split(jax.random.key(seed), 4)
    part_splits = jax.random.split(jax.random.fold_in(seeds[3], part), 4)
    return {
        "records": draw_records(jax.random.fold_in(jax.random.fold_in(seeds[3], part), 71), part),
        "dead_mask": touch_ends((jax.random.randint(part_splits[1], (NCH,), 0, 16) < 1).astype(jnp.int32), jax.random.fold_in(part_splits[1], 1), 0, 1),
        "offsets": draw_offsets(jax.random.fold_in(jax.random.fold_in(seeds[3], part), 71), part),
    }


EPS = 1e-05
TWO_PI = 2.0 * math.pi

def reference(records, dead_mask, offsets):
    channels = records.shape[0]
    live_samples = records * (1 - dead_mask).astype(jnp.float32)[:, None]
    box_sum = lax.reduce_window(jnp.abs(live_samples), jnp.float32(0.0), lax.add, (1, 2 * H + 1), (1, 1), ((0, 0), (H, H)))
    mean_level = box_sum / (2 * H + 1)
    normalised = live_samples / (mean_level + EPS)
    padded = jnp.pad(normalised, ((0, 0), (0, L)))
    taper_weights = 0.5 - 0.5 * jnp.cos(jnp.arange(L, dtype=jnp.int32).astype(jnp.float32) * (TWO_PI / L))
    bin_index = jnp.arange(NF, dtype=jnp.int32)
    freq_bins = K0 + bin_index
    band_matrix = (jnp.abs(bin_index[:, None] - bin_index[None, :]) <= WB).astype(jnp.float32)
    band_counts = lax.optimization_barrier(jnp.sum(band_matrix, axis=0))

    def spectrum(window_id):
        start = (window_id * HOP + offsets[window_id]).astype(jnp.int32)
        segment = lax.dynamic_slice_in_dim(padded, start, L, 1) * taper_weights
        full_spec = jnp.fft.rfft(segment, axis=1)[:, K0:K0 + NF]
        spec_real = jnp.real(full_spec).astype(jnp.float32)
        spec_imag = jnp.imag(full_spec).astype(jnp.float32)
        magnitude = jnp.sqrt(spec_real * spec_real + spec_imag * spec_imag + 1e-12)
        smoothed = jnp.dot(magnitude, band_matrix, precision=lax.Precision.HIGHEST, preferred_element_type=jnp.float32) / band_counts
        white_real = (spec_real / (smoothed + EPS)).astype(jnp.bfloat16)
        white_imag = (spec_imag / (smoothed + EPS)).astype(jnp.bfloat16)
        return (white_real, white_imag)
    white_real, white_imag = lax.map(spectrum, jnp.arange(NWIN, dtype=jnp.int32))
    real_cw = jnp.transpose(white_real, (1, 0, 2))
    imag_cw = jnp.transpose(white_imag, (1, 0, 2))
    features = jnp.stack([real_cw, imag_cw], axis=1).reshape(channels, 2 * NWIN * NF)
    padded_features = jnp.concatenate([features, jnp.zeros((NPART, 2 * NWIN * NF), jnp.bfloat16)], axis=0)
    own_real = real_cw.astype(jnp.float32)
    own_imag = imag_cw.astype(jnp.float32)
    lag_values = jnp.arange(NLAG, dtype=jnp.int32) - NLAG // 2
    lag_angle = jnp.mod(lag_values[:, None] * freq_bins[None, :], L).astype(jnp.float32) * (TWO_PI / L)
    cos_lag = jnp.cos(lag_angle)[:, None, None, :]
    sin_lag = jnp.sin(lag_angle)[:, None, None, :]
    norm_scale = 1.0 / math.sqrt(2.0 * NF * NWIN)
    block_rows = math.gcd(channels, 128)
    col_count = block_rows + NPART

    def block_corr(block_id):
        begin = (block_id * block_rows).astype(jnp.int32)
        block_real = lax.dynamic_slice_in_dim(own_real, begin, block_rows, 0)[None]
        block_imag = lax.dynamic_slice_in_dim(own_imag, begin, block_rows, 0)[None]
        rotated_real = block_real * cos_lag - block_imag * sin_lag
        rotated_imag = block_real * sin_lag + block_imag * cos_lag
        lag_rows = jnp.stack([rotated_real, rotated_imag], axis=2).astype(jnp.bfloat16).reshape(NLAG * block_rows, 2 * NWIN * NF)
        partners = lax.dynamic_slice_in_dim(padded_features, begin, col_count, 0)
        products = jnp.dot(lag_rows.astype(jnp.float32), partners.astype(jnp.float32).T, preferred_element_type=jnp.float32) * norm_scale
        flattened = products.reshape(NLAG, block_rows * col_count)[:, 1:]
        flattened = jnp.pad(flattened, ((0, 0), (0, block_rows + 1)))
        return flattened.reshape(NLAG, block_rows, col_count + 1)[:, :, :NPART].astype(jnp.bfloat16)
    lag_blocks = lax.map(block_corr, jnp.arange(channels // block_rows, dtype=jnp.int32))
    return jnp.transpose(lag_blocks, (1, 0, 2, 3)).reshape(NLAG, channels, NPART)
```

```python
import functools
import math

import jax
import jax.numpy as jnp
import numpy as np
from jax import lax
from jax.experimental import pallas as pl
from jax.experimental.pallas import tpu as pltpu
from jax.sharding import PartitionSpec as P

L = 8192
HOP = 4096
JIT = 512
H = 128
K0 = 32
NF = 256
WB = 64
NLAG = 32
NPART = 256

EPS = 1e-05
BLK = 256
SUB = 512
HALF = L // 2
NSUB = HALF // SUB
HB = NF // 2
ROWS = 16
CW = 2
CHUNK = 2 * CW * NF
MESH = pl.DeviceIdType.MESH
BF = jnp.bfloat16
F32 = jnp.float32

BINS = np.concatenate([np.arange(0, NF, 2), np.arange(1, NF, 2)])


def split_np(value):
    high = value.astype(jnp.bfloat16)
    low = (value - high.astype(np.float64)).astype(jnp.bfloat16)
    return high, low


def transform_tables():
    tables = []
    for parity in range(2):
        k = K0 + np.arange(parity, NF, 2)
        angle = 2 * np.pi * ((np.arange(SUB)[:, None] * k[None, :]) % L) / L
        tables.extend(split_np(np.concatenate([np.cos(angle), -np.sin(angle)], axis=1)))
    return tables


def twiddle_table():
    rows = []
    for parity in range(2):
        k = K0 + np.arange(parity, NF, 2)
        for a in range(NSUB):
            angle = 2 * np.pi * ((SUB * a * k) % L) / L
            rows.append(0.5 * np.cos(angle))
            rows.append(0.5 * np.sin(angle))
    return np.stack(rows).astype(np.float32)


def box_table():
    i = np.arange(BLK + 2 * H)[:, None]
    j = np.arange(BLK)[None, :] + H
    return (np.abs(i - j) <= H).astype(jnp.bfloat16)


def taper_table():
    angle = 2 * np.pi * np.arange(HALF) / L
    return np.stack([np.cos(angle), np.sin(angle)]).astype(np.float32)


def band_table():
    return (np.abs(BINS[:, None] - BINS[None, :]) <= WB).astype(jnp.bfloat16)


def bin_table():
    q = np.arange(NF)
    counts = (np.abs(q[:, None] - q[None, :]) <= WB).sum(axis=0)[BINS]
    return np.stack([K0 + BINS, counts]).astype(np.int32)


def split(value):
    high = value.astype(BF)
    return high, (value - high.astype(F32)).astype(BF)


def mm(a, b):
    return jnp.dot(a, b, preferred_element_type=F32)


def spectra_group(padded, blocks, windows, group, prepare, store, hook, x_ref, dead_ref, off_ref, box_ref,
                  taper_ref, te_hi, te_lo, to_hi, to_lo, tw_ref, band_ref, bin_ref, norm, cosw, turn, e_hi,
                  e_lo, o_hi, o_lo, ye, yo):
    tail = norm.shape[0] - blocks * ROWS

    @pl.when(prepare)
    def _():
        window = lax.broadcasted_iota(jnp.int32, (windows, 1), 0)
        off = jnp.zeros((windows, 1), jnp.int32)
        for w in range(windows):
            off = jnp.where(window == w, off_ref[w], off)
        angle = off.astype(F32) * (2.0 * math.pi / L)
        cosw[...] = taper_ref[0:1, :] * jnp.cos(angle) + taper_ref[1:2, :] * jnp.sin(angle)
        turns = ((off * bin_ref[0:1, :]) & (L - 1)).astype(F32) * (2.0 * math.pi / L)
        turn[0] = jnp.cos(turns)
        turn[1] = jnp.sin(turns)
        if tail:
            norm[blocks * ROWS:, :] = jnp.zeros((tail, BLK), F32)

    channel = lax.broadcasted_iota(jnp.int32, (ROWS, 1), 0)
    dead = jnp.zeros((ROWS, 1), jnp.int32)
    for c in range(ROWS):
        dead = jnp.where(channel == c, dead_ref[group * ROWS + c], dead)
    alive = (1 - dead).astype(F32)
    per = 16
    shift = H if padded else 0

    def normalise(first, count, left_edge, right_edge):
        mags, vals = [], []
        for i in range(count):
            base = (first + i) * BLK + shift
            at = base if isinstance(base, int) else pl.multiple_of(base, 128)
            vals.append(x_ref[:, pl.ds(at, BLK)] * alive)
            pieces = []
            lo = base - H if isinstance(base, int) else pl.multiple_of(base - H, 128)
            if left_edge and i == 0:
                pieces = [jnp.zeros((ROWS, H), F32), x_ref[:, pl.ds(at, BLK + H)]]
            elif right_edge and i == count - 1:
                pieces = [x_ref[:, pl.ds(lo, BLK + H)], jnp.zeros((ROWS, H), F32)]
            else:
                pieces = [x_ref[:, pl.ds(lo, BLK + 2 * H)]]
            piece = pieces[0] if len(pieces) == 1 else jnp.concatenate(pieces, axis=1)
            mags.append(jnp.abs(piece * alive).astype(BF))
        level = mm(jnp.concatenate(mags, axis=0), box_ref[...]) * (1.0 / (2 * H + 1))
        value = jnp.concatenate(vals, axis=0) / (level + EPS)
        at = first * ROWS if isinstance(first, int) else pl.multiple_of(first * ROWS, ROWS)
        norm[pl.ds(at, count * ROWS), :] = value

    if padded:
        full = blocks // per

        @pl.loop(0, full)
        def _(i):
            normalise(i * per, per, False, False)

        if blocks % per:
            normalise(full * per, blocks % per, False, False)
    else:
        normalise(0, per, True, blocks == per)

        @pl.loop(1, blocks // per - 1)
        def _(i):
            normalise(i * per, per, False, False)

        if blocks > per:
            normalise(blocks - per, per, False, True)

    lane = lax.broadcasted_iota(jnp.int32, (ROWS, BLK), 1)
    hop_blocks = HOP // BLK

    @pl.loop(0, windows)
    def _(w):
        base = w * hop_blocks

        def block(i):
            return norm[pl.ds(pl.multiple_of((base + i) * ROWS, ROWS), ROWS), :]

        off_w = off_ref[w]
        for a in range(NSUB):
            for h in range(SUB // BLK):
                i = a * (SUB // BLK) + h
                first = block(i)
                if i * BLK < JIT:
                    first = jnp.where(lane + i * BLK < off_w, block(i + 2 * hop_blocks), first)
                second = block(i + hop_blocks)
                cosine = cosw[pl.ds(w, 1), i * BLK:(i + 1) * BLK]
                total, delta = first + second, first - second
                cols = slice(h * BLK, (h + 1) * BLK)
                at = pl.ds(pl.multiple_of((w * NSUB + a) * ROWS, ROWS), ROWS)
                e_hi[at, cols], e_lo[at, cols] = split(total - cosine * delta)
                o_hi[at, cols], o_lo[at, cols] = split(delta - cosine * total)

    hook(0)
    ye[...] = mm(e_hi[...], te_hi[...]) + mm(e_hi[...], te_lo[...]) + mm(e_lo[...], te_hi[...])
    hook(1)
    yo[...] = mm(o_hi[...], to_hi[...]) + mm(o_hi[...], to_lo[...]) + mm(o_lo[...], to_hi[...])

    hook(2)
    inverse = 1.0 / bin_ref[1:2, :].astype(F32)
    reals, imags = [], []
    for w in range(windows):
        parts = []
        for parity, y in ((0, ye), (1, yo)):
            real = imag = None
            for a in range(NSUB):
                at = (w * NSUB + a) * ROWS
                yr, yi = y[at:at + ROWS, :HB], y[at:at + ROWS, HB:]
                row = (parity * NSUB + a) * 2
                c, s = tw_ref[row:row + 1, :], tw_ref[row + 1:row + 2, :]
                r, m = yr * c + yi * s, yi * c - yr * s
                real, imag = (r, m) if real is None else (real + r, imag + m)
            parts.append((real, imag))
        real = jnp.concatenate([parts[0][0], parts[1][0]], axis=1)
        imag = jnp.concatenate([parts[0][1], parts[1][1]], axis=1)
        c, s = turn[0, w:w + 1, :], turn[1, w:w + 1, :]
        reals.append(real * c - imag * s)
        imags.append(real * s + imag * c)
    real, imag = jnp.concatenate(reals, axis=0), jnp.concatenate(imags, axis=0)
    mag_hi, mag_lo = split(jnp.sqrt(real * real + imag * imag + 1e-12))
    smooth = (mm(mag_hi, band_ref[...]) + mm(mag_lo, band_ref[...])) * inverse + EPS
    white = ((real / smooth).astype(BF), (imag / smooth).astype(BF))
    for part in range(2):
        for w in range(windows):
            at = (part * CW + w % CW) * NF
            store(w // CW, at, white[part][w * ROWS:(w + 1) * ROWS, :])


def spectra_kernel(padded, blocks, windows, x_ref, dead_ref, off_ref, *refs):
    out_ref = refs[9]

    def store(k, at, value):
        out_ref[k, :, at:at + NF] = value

    spectra_group(padded, blocks, windows, pl.program_id(0), pl.program_id(0) == 0, store, lambda stage: None,
                  x_ref, dead_ref, off_ref, *refs[:9], *refs[10:])


def spectra_consts():
    tables = [box_table(), taper_table(), *transform_tables(), twiddle_table(), band_table(), bin_table()]
    return [jnp.asarray(t) for t in tables]


def spectra_scratch(norm_blocks, windows):
    rows = windows * NSUB * ROWS
    return [
        pltpu.VMEM((norm_blocks * ROWS, BLK), F32),
        pltpu.VMEM((windows, HALF), F32),
        pltpu.VMEM((2, windows, NF), F32),
    ] + [pltpu.VMEM((rows, SUB), BF)] * 4 + [pltpu.VMEM((rows, NF), F32)] * 2


def spectra(samples_in, dead_mask, offsets, padded, samples, windows):
    channels, width = samples_in.shape
    blocks = (samples + (HOP + JIT if padded else 0)) // BLK
    norm_blocks = (samples + HOP + JIT) // BLK
    consts = spectra_consts()
    whole = [pl.BlockSpec(c.shape, lambda i: (0, 0)) for c in consts]
    return pl.pallas_call(
        functools.partial(spectra_kernel, padded, blocks, windows),
        grid=(channels // ROWS,),
        out_shape=jax.ShapeDtypeStruct((windows // CW, channels, CHUNK), BF),
        in_specs=[
            pl.BlockSpec((ROWS, width), lambda i: (i, 0)),
            pl.BlockSpec(memory_space=pltpu.SMEM),
            pl.BlockSpec(memory_space=pltpu.SMEM),
        ] + whole,
        out_specs=pl.BlockSpec((windows // CW, ROWS, CHUNK), lambda i: (0, i, 0)),
        scratch_shapes=spectra_scratch(norm_blocks, windows),
        compiler_params=pltpu.CompilerParams(vmem_limit_bytes=56 << 20),
        name="spectra",
    )(samples_in, dead_mask, offsets, *consts)


def lag_table():
    lags = np.arange(NLAG) - NLAG // 2
    angle = 2 * np.pi * ((lags[:, None] * (K0 + BINS)[None, :]) % L) / L
    return np.stack([np.cos(angle), np.sin(angle)]).astype(np.float32)


GROUP = 8


def correlate_kernel(scale, devices, produce, own_ref, lag_ref, out_ref, feats, rot, total, send, recv):
    _, chunks, channels, _ = feats.shape
    per = chunks // 2
    groups = channels // ROWS
    units = 2 * groups
    lags = out_ref.shape[0]
    i = lax.axis_index("chan")
    r = lax.rem(i, 4)
    x, c = r // 2, lax.rem(r, 2)
    has_prev, has_next, has_third = i >= 4, i + 4 < devices, i + 8 < devices
    prev, following = i - 4, i + 4
    across, partner = i + 2 - 4 * x, i + 1 - 2 * c

    barrier = pltpu.get_barrier_semaphore()

    def greet(device):
        pl.semaphore_signal(barrier, inc=1, device_id={"chan": device}, device_id_type=MESH)

    greet(across)
    greet(partner)
    pl.when(has_prev)(lambda: greet(prev))
    pl.when(has_next)(lambda: greet(following))

    def all_here():
        pl.semaphore_wait(barrier, 2 + has_prev.astype(jnp.int32) + has_next.astype(jnp.int32))

    def unit(slot, k):
        return feats.at[slot, pl.ds(k % 2 * per, per), pl.ds(k // 2 * ROWS, ROWS)]

    def copy(item, k, source, slot, device):
        return pltpu.make_async_remote_copy(
            src_ref=unit(source, k),
            dst_ref=unit(slot, k),
            send_sem=send.at[item, k],
            recv_sem=recv.at[slot, k],
            device_id={"chan": device},
            device_id_type=MESH,
        )

    def arrived(slot, k):
        pltpu.make_async_copy(unit(slot, k), unit(slot, k), recv.at[slot, k]).wait()

    def left(item, k):
        pltpu.make_async_copy(unit(0, k), unit(0, k), send.at[item, k]).wait()

    def send_own(k):
        pl.when(has_prev)(lambda: copy(0, k, 0, 4, prev).start())
        pl.when(x == 1)(lambda: copy(2, k, 0, 2, across).start())
        pl.when(c == 1)(lambda: copy(4, k, 0, 1, partner).start())

    def first_forward(k):
        @pl.when(has_next)
        def _():
            arrived(4, k)
            pl.when(has_prev)(lambda: copy(1, k, 4, 8, prev).start())
            copy(2 + x, k, 4, 2 + 4 * x, across).start()
            copy(4 + c, k, 4, 3 + 2 * c, partner).start()

    def first_relay(k):
        @pl.when(i + 2 < devices)
        def _():
            arrived(2, k)
            copy(6, k, 2, 1 + 2 * c, partner).start()

    def last_forward(k):
        @pl.when(has_third)
        def _():
            arrived(8, k)
            pl.when(x == 0)(lambda: copy(3, k, 8, 6, across).start())
            pl.when(c == 0)(lambda: copy(5, k, 8, 7, partner).start())

    def last_relay(k):
        @pl.when(i + 6 < devices)
        def _():
            arrived(6, k)
            copy(7, k, 6, 5 + 2 * c, partner).start()

    for slot in range(1, 9):
        @pl.when(i + slot >= devices)
        def _(slot=slot):
            feats[slot] = jnp.zeros(feats.shape[1:], BF)

    size = GROUP * channels
    row = lax.broadcasted_iota(jnp.int32, (size, size), 0)
    col = lax.broadcasted_iota(jnp.int32, (size, size), 1)
    within = lax.rem(row, channels)
    flip = (col == row - within + (channels - 1 - within)).astype(F32).astype(BF)

    def rotate(k):
        backward = mm(flip[:channels, :channels], feats[0, k])
        for w in range(CW):
            lo, hi = w * NF, (CW + w) * NF
            real, imag = backward[:, lo:lo + NF], backward[:, hi:hi + NF]

            @pl.loop(0, lags, unroll=4)
            def _(t):
                co, si = lag_ref[0, pl.ds(t, 1), :], lag_ref[1, pl.ds(t, 1), :]
                at = pl.ds(pl.multiple_of(t * channels, channels), channels)
                rot[k, at, lo:lo + NF] = (real * co - imag * si).astype(BF)
                rot[k, at, hi:hi + NF] = (real * si + imag * co).astype(BF)

    def multiply(k):
        products = lax.dot_general(
            rot[k], feats[:, k].reshape(9 * channels, CHUNK), (((1,), (1,)), ((), ())),
            preferred_element_type=F32)
        if k == 0:
            total[...] = products
        elif k < chunks - 1:
            total[...] += products
        else:
            total[...] = (total[...] + products) * scale

    def odd_arrived(k):
        for slot in (1, 3, 5, 7):
            pl.when(i + slot < devices)(lambda slot=slot: arrived(slot, k))

    if produce is None:
        all_here()
        for k in range(chunks):
            feats[0, k] = own_ref[k]
        for k in range(units):
            send_own(k)
        early = 0
    else:
        def stages(stage):
            if stage < 2:
                first_forward(stage)
            else:
                first_relay(0)
                first_relay(1)

        produce(0, lambda stage: None)
        all_here()
        send_own(0)
        send_own(1)
        for group in range(1, groups):
            produce(group, stages if group == 1 else lambda stage: None)
            send_own(2 * group)
            send_own(2 * group + 1)
        early = 2
    turns = iter(range(chunks))

    def turn_some(count):
        for _ in range(count):
            k = next(turns, None)
            if k is not None:
                rotate(k)

    for k in range(early):
        last_forward(k)
    for k in range(early):
        last_relay(k)
    share = -(-chunks // max(1, units - early))
    for k in range(early, units):
        turn_some(share)
        first_forward(k)
    turn_some(chunks)
    for k in range(early, units):
        first_relay(k)
    for k in range(early):
        odd_arrived(k)
    for k in range(early, units):
        last_forward(k)
        if k > early:
            last_relay(k - 1)
    last_relay(units - 1)
    for half in range(2):
        for group in range(groups):
            if 2 * group + half >= early:
                odd_arrived(2 * group + half)
        for k in range(half * per, (half + 1) * per):
            multiply(k)

    cols = total.shape[1]
    wide = -(-cols // 128) * 128

    @pl.loop(0, lags // GROUP)
    def _(g):
        pieces = []
        for t in range(GROUP):
            at = pl.multiple_of((g * GROUP + t) * channels, channels)
            piece = total[pl.ds(at, channels), :]
            piece = jnp.concatenate([piece, jnp.zeros((channels, wide - cols), F32)], axis=1)
            piece = pltpu.roll(piece, wide - channels, 1, stride=1, stride_axis=0)
            pieces.append(piece[:, :NPART].astype(BF))
        result = mm(flip, jnp.concatenate(pieces, axis=0)).astype(BF)
        for t in range(GROUP):
            out_ref[g * GROUP + t] = result[t * channels:(t + 1) * channels, :]

    for k in range(units):
        pl.when(has_prev)(lambda k=k: left(0, k))
        pl.when(has_prev & has_next)(lambda k=k: left(1, k))
        for item, source in ((2, 4 - 4 * x), (3, 8 - 4 * x), (4, 4 - 4 * c), (5, 8 - 4 * c), (6, 2), (7, 6)):
            pl.when(i + source < devices)(lambda item=item, k=k: left(item, k))


def correlate_call(kernel, operands, specs, count, channels, chunks, extra):
    units = 2 * (channels // ROWS)
    return pl.pallas_call(
        kernel,
        out_shape=jax.ShapeDtypeStruct((count, channels, NPART), BF),
        in_specs=specs,
        out_specs=pl.BlockSpec(memory_space=pltpu.VMEM),
        scratch_shapes=[
            pltpu.VMEM((9, chunks, channels, CHUNK), BF),
            pltpu.VMEM((chunks, count * channels, CHUNK), BF),
            pltpu.VMEM((count * channels, 9 * channels), F32),
            pltpu.SemaphoreType.DMA((8, units)),
            pltpu.SemaphoreType.DMA((9, units)),
        ] + extra,
        compiler_params=pltpu.CompilerParams(
            collective_id=0, has_side_effects=True, vmem_limit_bytes=56 << 20),
        name="correlate",
    )(*operands)


def scale_of(chunks):
    return 1.0 / math.sqrt(2.0 * NF * chunks * CW)


def correlate(own, lags, devices):
    chunks, channels, _ = own.shape
    kernel = functools.partial(correlate_kernel, scale_of(chunks), devices, None)
    specs = [pl.BlockSpec(memory_space=pltpu.VMEM)] * 2
    return correlate_call(kernel, (own, lags), specs, lags.shape[1], channels, chunks, [])


def prepare_windows(windows, off_ref, taper_ref, bin_ref, cosw, turn):
    for w in range(windows):
        angle = jnp.full((8, 1), off_ref[w], jnp.int32).astype(F32) * (2.0 * math.pi / L)
        at = slice(8 * w, 8 * w + 8)
        cosw[at, :] = taper_ref[0:1, :] * jnp.cos(angle) + taper_ref[1:2, :] * jnp.sin(angle)
        turns = ((off_ref[w] * bin_ref[0:1, :]) & (L - 1)).astype(F32) * (2.0 * math.pi / L)
        turn[0, at, :] = jnp.broadcast_to(jnp.cos(turns), (8, NF))
        turn[1, at, :] = jnp.broadcast_to(jnp.sin(turns), (8, NF))


def repeat_rows(value, rows):
    return jnp.concatenate([value] * (rows // value.shape[0]), axis=0)


def window_spectra(w, hook, alive, off_ref, box_ref, te_hi, te_lo, to_hi, to_lo, tw_ref, band_ref, bin_ref, held, mags,
                   norm, cosw, turn, e_hi, e_lo, o_hi, o_lo):
    channels = held.shape[0]
    hop_blocks = HOP // BLK
    base = pl.multiple_of(w * HOP, HOP)

    def cols(first, count):
        return pl.ds(pl.multiple_of(base + first, 128), count)

    mags[:, cols(0, HOP)] = jnp.abs(held[:, cols(0, HOP)]).astype(BF)
    pieces = [mags[:, cols(b * BLK, BLK + 2 * H)] for b in range(hop_blocks)]
    level = mm(jnp.concatenate(pieces, axis=0), box_ref[...]) * (1.0 / (2 * H + 1)) + EPS
    values = jnp.concatenate([held[:, cols(H + b * BLK, BLK)] for b in range(hop_blocks)], axis=0)
    rows = hop_blocks * channels
    norm[pl.ds(pl.multiple_of(w * rows, rows), rows), :] = values / level

    def block(i):
        return norm[pl.ds(pl.multiple_of((w * hop_blocks + i) * channels, channels), channels), :]

    hook()
    lane = lax.broadcasted_iota(jnp.int32, (channels, BLK), 1)
    off_w = off_ref[w]
    per_w = pl.ds(pl.multiple_of(8 * w, 8), 8)
    for a in range(NSUB):
        for h in range(SUB // BLK):
            i = a * (SUB // BLK) + h
            first = block(i)
            if i * BLK < JIT:
                first = jnp.where(lane + i * BLK < off_w, block(i + 2 * hop_blocks), first)
            second = block(i + hop_blocks)
            cosine = repeat_rows(cosw[per_w, i * BLK:(i + 1) * BLK], channels)
            total, delta = first + second, first - second
            at, span = slice(a * channels, (a + 1) * channels), slice(h * BLK, (h + 1) * BLK)
            e_hi[at, span], e_lo[at, span] = split(total - cosine * delta)
            o_hi[at, span], o_lo[at, span] = split(delta - cosine * total)

    parts = []
    for parity, (hi, lo, t_hi, t_lo) in enumerate(((e_hi, e_lo, te_hi, te_lo), (o_hi, o_lo, to_hi, to_lo))):
        y = mm(jnp.concatenate([hi[...], hi[...], lo[...]], axis=1),
               jnp.concatenate([t_hi[...], t_lo[...], t_hi[...]], axis=0))
        real = imag = None
        for a in range(NSUB):
            at = slice(a * channels, (a + 1) * channels)
            yr, yi = y[at, :HB], y[at, HB:]
            row = (parity * NSUB + a) * 2
            c, s = tw_ref[row:row + 1, :], tw_ref[row + 1:row + 2, :]
            r, m = yr * c + yi * s, yi * c - yr * s
            real, imag = (r, m) if real is None else (real + r, imag + m)
        parts.append((real, imag))
    real = jnp.concatenate([parts[0][0], parts[1][0]], axis=1)
    imag = jnp.concatenate([parts[0][1], parts[1][1]], axis=1)
    c, s = repeat_rows(turn[0, per_w, :], channels), repeat_rows(turn[1, per_w, :], channels)
    real, imag = real * c - imag * s, real * s + imag * c
    mag_hi, mag_lo = split(jnp.sqrt(real * real + imag * imag + 1e-12))
    inverse = 1.0 / bin_ref[1:2, :].astype(F32)
    smooth = (mm(mag_hi, band_ref[...]) + mm(mag_lo, band_ref[...])) * inverse + EPS
    return (real / smooth * alive).astype(BF), (imag / smooth * alive).astype(BF)


def whole_kernel(scale, devices, windows, records, dead_ref, off_ref, box_ref, taper_ref, te_hi, te_lo, to_hi, to_lo,
                 tw_ref, band_ref, bin_ref, lag_ref, out_ref, feats, rot, total, own, staged, send, recv, held, loaded,
                 stored, mags, norm, cosw, turn, e_hi, e_lo, o_hi, o_lo):
    channels, samples = records.shape
    lags = lag_ref.shape[1]
    half = lags // 2
    i = lax.axis_index("chan")
    r = lax.rem(i, 4)
    x, c = r // 2, lax.rem(r, 2)
    has_prev, has_next, has_third = i >= 4, i + 4 < devices, i + 8 < devices
    prev, following = i - 4, i + 4
    across, partner = i + 2 - 4 * x, i + 1 - 2 * c

    def load(w):
        first = max(0, w * HOP - H)
        last = (w + 1) * HOP - H if w < windows - 1 else samples
        return pltpu.make_async_copy(
            records.at[:, pl.ds(first, last - first)], held.at[:, pl.ds(first + H, last - first)], loaded.at[w])

    for w in reversed(range(windows)):
        load(w).start()

    barrier = pltpu.get_barrier_semaphore()

    def greet(device):
        pl.semaphore_signal(barrier, inc=1, device_id={"chan": device}, device_id_type=MESH)

    greet(across)
    greet(partner)
    pl.when(has_prev)(lambda: greet(prev))
    pl.when(has_next)(lambda: greet(following))

    def all_here():
        pl.semaphore_wait(barrier, 2 + has_prev.astype(jnp.int32) + has_next.astype(jnp.int32))

    def copy(item, k, source, slot, device):
        return pltpu.make_async_remote_copy(
            src_ref=feats.at[source, k],
            dst_ref=feats.at[slot, k],
            send_sem=send.at[item, k],
            recv_sem=recv.at[slot, k],
            device_id={"chan": device},
            device_id_type=MESH,
        )

    def arrived(slot, k):
        pltpu.make_async_copy(feats.at[slot, k], feats.at[slot, k], recv.at[slot, k]).wait()

    def left(item, k):
        pltpu.make_async_copy(feats.at[0, k], feats.at[0, k], send.at[item, k]).wait()

    def send_own(k):
        pl.when(has_prev)(lambda: copy(0, k, 0, 4, prev).start())
        pl.when(x == 1)(lambda: copy(2, k, 0, 2, across).start())
        pl.when(c == 1)(lambda: copy(4, k, 0, 1, partner).start())

    def forward_next(k, here):
        @pl.when(here & has_next)
        def _():
            arrived(4, k)
            pl.when(has_prev)(lambda: copy(1, k, 4, 8, prev).start())
            copy(2 + x, k, 4, 2 + 4 * x, across).start()
            copy(4 + c, k, 4, 3 + 2 * c, partner).start()

    def relay_near(k, here):
        @pl.when(here & (i + 2 < devices))
        def _():
            arrived(2, k)
            copy(6, k, 2, 1 + 2 * c, partner).start()

    def forward_third(k, here):
        @pl.when(here & has_third)
        def _():
            arrived(8, k)
            pl.when(x == 0)(lambda: copy(3, k, 8, 6, across).start())
            pl.when(c == 0)(lambda: copy(5, k, 8, 7, partner).start())

    def relay_far(k, here):
        @pl.when(here & (i + 6 < devices))
        def _():
            arrived(6, k)
            copy(7, k, 6, 5 + 2 * c, partner).start()

    def there(k):
        return (k >= 0) & (k < windows)

    def mid_tick(n):
        forward_next(n - 3, there(n - 3))
        relay_near(n - 3, there(n - 3) & (x == 0))
        relay_far(n - 8, there(n - 8) & (x == 1))

    def end_tick(n):
        forward_third(n - 5, there(n - 5))
        relay_near(n - 5, there(n - 5) & (x == 1))
        relay_far(n - 5, there(n - 5) & (x == 0))

    for slot in range(1, 9):
        @pl.when(i + slot >= devices)
        def _(slot=slot):
            feats[slot] = jnp.zeros(feats.shape[1:], BF)

    size = GROUP * channels
    row = lax.broadcasted_iota(jnp.int32, (size, size), 0)
    col = lax.broadcasted_iota(jnp.int32, (size, size), 1)
    within = lax.rem(row, channels)
    flip = (col == row - within + (channels - 1 - within)).astype(F32).astype(BF)

    def rotate(k):
        backward = mm(flip[:channels, :channels], feats[0, k])
        real, imag = backward[:, :NF], backward[:, NF:]

        def put(t, a, b):
            rot[k, t * channels:(t + 1) * channels, :NF] = a.astype(BF)
            rot[k, t * channels:(t + 1) * channels, NF:] = b.astype(BF)

        put(half, real, imag)
        for step in range(1, half + 1):
            t = half - step
            co, si = lag_ref[0, t:t + 1, :], lag_ref[1, t:t + 1, :]
            rc, rs, ic, js = real * co, real * si, imag * co, imag * si
            put(t, rc - js, rs + ic)
            if half + step < lags:
                put(half + step, rc + js, ic - rs)

    def side(ref, units):
        return jnp.concatenate([ref(k) for k in units], axis=1)

    def product(units, columns):
        return lax.dot_general(
            side(lambda k: rot[k], units), side(columns, units), (((1,), (1,)), ((), ())),
            preferred_element_type=F32)

    def own_columns(k):
        return jnp.concatenate([jnp.zeros((128 - channels, 2 * NF), BF), feats[0, k]], axis=0)

    def far_columns(k):
        return feats[1:9, k].reshape(8 * channels, 2 * NF)

    def multiply(units):
        for k in units:
            for slot in (1, 3, 5, 7):
                pl.when(i + slot < devices)(lambda slot=slot, k=k: arrived(slot, k))
        products = product(units, far_columns)
        if units[0] == 0:
            total[...] = products
        else:
            total[...] += products

    def own_multiply(units):
        pl.loop(units[0], units[-1] + 1)(rotate)
        products = product(units, own_columns)
        if units[0] == 0:
            own[...] = products
        else:
            own[...] += products

    channel = lax.broadcasted_iota(jnp.int32, (channels, 1), 0)
    dead = jnp.zeros((channels, 1), jnp.int32)
    for j in range(channels):
        dead = jnp.where(channel == j, dead_ref[j], dead)
    alive = (1 - dead).astype(F32)
    prepare_windows(windows, off_ref, taper_ref, bin_ref, cosw, turn)
    held[:, :H] = jnp.zeros((channels, H), F32)
    held[:, samples + H:] = jnp.zeros((channels, H), F32)
    tail = samples // BLK * channels
    norm[tail:, :] = jnp.zeros((norm.shape[0] - tail, BLK), F32)
    load(windows - 1).wait()
    all_here()
    mags[:, samples:] = jnp.abs(held[:, samples:]).astype(BF)

    @pl.loop(0, windows)
    def _(n):
        w = windows - 1 - n
        pl.when(w == 0)(lambda: load(0).wait())
        if windows > 2:
            pl.when((w > 0) & (n > 0))(lambda: pltpu.make_async_copy(
                records.at[:, pl.ds(H, HOP)], held.at[:, pl.ds(H, HOP)], loaded.at[w]).wait())
        real, imag = window_spectra(
            w, lambda: mid_tick(n), alive, off_ref, box_ref, te_hi, te_lo, to_hi, to_lo, tw_ref, band_ref, bin_ref, held, mags,
            norm, cosw, turn, e_hi, e_lo, o_hi, o_lo)
        feats[0, n, :, :NF] = real
        feats[0, n, :, NF:] = imag
        send_own(n)
        end_tick(n)

    pairs = [range(k, k + 2) for k in range(0, windows, 2)]
    early = [[k for pair in pairs[:-2] for k in pair], pairs[-2], pairs[-1][:1]]
    tasks = [lambda p=p: own_multiply(p) for p in pairs] + [lambda p=p: multiply(p) for p in early]
    for n in range(windows, windows + 8):
        mid_tick(n)
        if tasks:
            tasks.pop(0)()
        end_tick(n)
    for task in tasks:
        task()
    multiply(pairs[-1][1:])

    def store(g):
        at = pl.ds(g * GROUP, GROUP)
        return pltpu.make_async_copy(staged.at[at], out_ref.at[at], stored.at[g])

    for g in range(lags // GROUP):
        pieces = []
        for t in range(GROUP):
            at = slice((g * GROUP + t) * channels, (g * GROUP + t + 1) * channels)
            piece = jnp.concatenate([total[at, :], own[at, :]], axis=1) * scale
            piece = pltpu.roll(piece, 0, 1, stride=1, stride_axis=0)
            pieces.append(piece[:, :NPART].astype(BF))
        result = mm(flip, jnp.concatenate(pieces, axis=0)).astype(BF)
        for t in range(GROUP):
            staged[g * GROUP + t] = result[t * channels:(t + 1) * channels, :]
        store(g).start()

    @pl.loop(0, windows)
    def _(k):
        pl.when(has_prev)(lambda: left(0, k))
        pl.when(has_prev & has_next)(lambda: left(1, k))
        for item, source in ((2, 4 - 4 * x), (3, 8 - 4 * x), (4, 4 - 4 * c), (5, 8 - 4 * c), (6, 2), (7, 6)):
            pl.when(i + source < devices)(lambda item=item: left(item, k))

    for g in range(lags // GROUP):
        store(g).wait()


def whole(records, dead_mask, offsets, lags, devices):
    channels, samples = records.shape
    windows = samples // HOP
    count = lags.shape[1]
    consts = spectra_consts()
    vmem, smem = pl.BlockSpec(memory_space=pltpu.VMEM), pl.BlockSpec(memory_space=pltpu.SMEM)
    rows = NSUB * channels
    return pl.pallas_call(
        functools.partial(whole_kernel, 1.0 / math.sqrt(2.0 * NF * windows), devices, windows),
        out_shape=jax.ShapeDtypeStruct((count, channels, NPART), BF),
        in_specs=[pl.BlockSpec(memory_space=pl.ANY), smem, smem] + [vmem] * (len(consts) + 1),
        out_specs=pl.BlockSpec(memory_space=pl.ANY),
        scratch_shapes=[
            pltpu.VMEM((9, windows, channels, 2 * NF), BF),
            pltpu.VMEM((windows, count * channels, 2 * NF), BF),
            pltpu.VMEM((count * channels, 8 * channels), F32),
            pltpu.VMEM((count * channels, 128), F32),
            pltpu.VMEM((count, channels, NPART), BF),
            pltpu.SemaphoreType.DMA((8, windows)),
            pltpu.SemaphoreType.DMA((9, windows)),
            pltpu.VMEM((channels, samples + 2 * H), F32),
            pltpu.SemaphoreType.DMA((windows,)),
            pltpu.SemaphoreType.DMA((count // GROUP,)),
            pltpu.VMEM((channels, samples + 2 * H), BF),
            pltpu.VMEM(((samples + HOP + JIT) // BLK * channels, BLK), F32),
            pltpu.VMEM((8 * windows, HALF), F32),
            pltpu.VMEM((2, 8 * windows, NF), F32),
        ] + [pltpu.VMEM((rows, SUB), BF)] * 4,
        compiler_params=pltpu.CompilerParams(
            collective_id=0, has_side_effects=True, vmem_limit_bytes=56 << 20),
        name="correlate",
    )(records, dead_mask, offsets, *consts, lags)


def shifted(value, axis, steps):
    count = lax.axis_size(axis)
    leading, last = (max(0, -steps), min(count, count - steps))
    return lax.ppermute(value, axis, [(source, source + steps) for source in range(leading, last)])


def local(records, dead_mask, offsets):
    channels, samples = records.shape
    tm_count = lax.axis_size("tm")
    tm_index = lax.axis_index("tm")
    windows = samples // HOP
    lags = jnp.asarray(lag_table())
    devices = lax.axis_size("chan")
    if tm_count == 1:
        return whole(records, dead_mask, offsets, lags, devices)
    left = shifted(records[:, -H:], "tm", 1)
    right = shifted(records[:, :HOP + JIT + H], "tm", -1)
    values = jnp.concatenate([left, records, right], axis=1)
    own_offsets = lax.dynamic_slice_in_dim(offsets, tm_index * windows, windows, 0)
    own = spectra(values, dead_mask, own_offsets, True, samples, windows)
    own = lax.all_gather(own, "tm", axis=0, tiled=True)
    lags_local = NLAG // tm_count
    lags = lax.dynamic_slice_in_dim(lags, tm_index * lags_local, lags_local, 1)
    return correlate(own, lags, devices)


def solution(mesh):
    return jax.shard_map(
        local,
        mesh=mesh,
        in_specs=(P(("win", "chan"), "tm"), P(("win", "chan")), P("win")),
        out_specs=P("tm", ("win", "chan"), None),
        check_vma=False,
    )
```

```python
import functools
import math

import jax
import jax.numpy as jnp
import numpy as np
from jax import lax
from jax.experimental import pallas as pl
from jax.experimental.pallas import tpu as pltpu
from jax.sharding import PartitionSpec as P

L = 8192
HOP = 4096
JIT = 512
H = 128
K0 = 32
NF = 256
WB = 64
NLAG = 32
NPART = 256

EPS = 1e-05
BLK = 256
SUB = 512
HALF = L // 2
NSUB = HALF // SUB
HB = NF // 2
ROWS = 16
CW = 2
CHUNK = 2 * CW * NF
MESH = pl.DeviceIdType.MESH
FIRST, SECOND, THIRD = 3, 5, 8
BF = jnp.bfloat16
F32 = jnp.float32

BINS = np.concatenate([np.arange(0, NF, 2), np.arange(1, NF, 2)])


def split_np(value):
    high = value.astype(jnp.bfloat16)
    low = (value - high.astype(np.float64)).astype(jnp.bfloat16)
    return high, low


def transform_tables():
    tables = []
    for parity in range(2):
        k = K0 + np.arange(parity, NF, 2)
        angle = 2 * np.pi * ((np.arange(SUB)[:, None] * k[None, :]) % L) / L
        tables.extend(split_np(np.concatenate([np.cos(angle), -np.sin(angle)], axis=1)))
    return tables


def twiddle_table():
    rows = []
    for parity in range(2):
        k = K0 + np.arange(parity, NF, 2)
        for a in range(NSUB):
            angle = 2 * np.pi * ((SUB * a * k) % L) / L
            rows.append(0.5 * np.cos(angle))
            rows.append(0.5 * np.sin(angle))
    return np.stack(rows).astype(np.float32)


def box_table():
    i = np.arange(BLK + 2 * H)[:, None]
    j = np.arange(BLK)[None, :] + H
    return (np.abs(i - j) <= H).astype(jnp.bfloat16)


def taper_table():
    angle = 2 * np.pi * np.arange(HALF) / L
    return np.stack([np.cos(angle), np.sin(angle)]).astype(np.float32)


def band_table():
    return (np.abs(BINS[:, None] - BINS[None, :]) <= WB).astype(jnp.bfloat16)


def bin_table():
    q = np.arange(NF)
    counts = (np.abs(q[:, None] - q[None, :]) <= WB).sum(axis=0)[BINS]
    return np.stack([K0 + BINS, counts]).astype(np.int32)


def split(value):
    high = value.astype(BF)
    return high, (value - high.astype(F32)).astype(BF)


def mm(a, b):
    return jnp.dot(a, b, preferred_element_type=F32)


def spectra_group(padded, blocks, windows, group, prepare, store, hook, x_ref, dead_ref, off_ref, box_ref,
                  taper_ref, te_hi, te_lo, to_hi, to_lo, tw_ref, band_ref, bin_ref, norm, cosw, turn, e_hi,
                  e_lo, o_hi, o_lo, ye, yo):
    tail = norm.shape[0] - blocks * ROWS

    @pl.when(prepare)
    def _():
        window = lax.broadcasted_iota(jnp.int32, (windows, 1), 0)
        off = jnp.zeros((windows, 1), jnp.int32)
        for w in range(windows):
            off = jnp.where(window == w, off_ref[w], off)
        angle = off.astype(F32) * (2.0 * math.pi / L)
        cosw[...] = taper_ref[0:1, :] * jnp.cos(angle) + taper_ref[1:2, :] * jnp.sin(angle)
        turns = ((off * bin_ref[0:1, :]) & (L - 1)).astype(F32) * (2.0 * math.pi / L)
        turn[0] = jnp.cos(turns)
        turn[1] = jnp.sin(turns)
        if tail:
            norm[blocks * ROWS:, :] = jnp.zeros((tail, BLK), F32)

    channel = lax.broadcasted_iota(jnp.int32, (ROWS, 1), 0)
    dead = jnp.zeros((ROWS, 1), jnp.int32)
    for c in range(ROWS):
        dead = jnp.where(channel == c, dead_ref[group * ROWS + c], dead)
    alive = (1 - dead).astype(F32)
    per = 16
    shift = H if padded else 0

    def normalise(first, count, left_edge, right_edge):
        mags, vals = [], []
        for i in range(count):
            base = (first + i) * BLK + shift
            at = base if isinstance(base, int) else pl.multiple_of(base, 128)
            vals.append(x_ref[:, pl.ds(at, BLK)] * alive)
            pieces = []
            lo = base - H if isinstance(base, int) else pl.multiple_of(base - H, 128)
            if left_edge and i == 0:
                pieces = [jnp.zeros((ROWS, H), F32), x_ref[:, pl.ds(at, BLK + H)]]
            elif right_edge and i == count - 1:
                pieces = [x_ref[:, pl.ds(lo, BLK + H)], jnp.zeros((ROWS, H), F32)]
            else:
                pieces = [x_ref[:, pl.ds(lo, BLK + 2 * H)]]
            piece = pieces[0] if len(pieces) == 1 else jnp.concatenate(pieces, axis=1)
            mags.append(jnp.abs(piece * alive).astype(BF))
        level = mm(jnp.concatenate(mags, axis=0), box_ref[...]) * (1.0 / (2 * H + 1))
        value = jnp.concatenate(vals, axis=0) / (level + EPS)
        at = first * ROWS if isinstance(first, int) else pl.multiple_of(first * ROWS, ROWS)
        norm[pl.ds(at, count * ROWS), :] = value

    if padded:
        full = blocks // per

        @pl.loop(0, full)
        def _(i):
            normalise(i * per, per, False, False)

        if blocks % per:
            normalise(full * per, blocks % per, False, False)
    else:
        normalise(0, per, True, blocks == per)

        @pl.loop(1, blocks // per - 1)
        def _(i):
            normalise(i * per, per, False, False)

        if blocks > per:
            normalise(blocks - per, per, False, True)

    lane = lax.broadcasted_iota(jnp.int32, (ROWS, BLK), 1)
    hop_blocks = HOP // BLK

    @pl.loop(0, windows)
    def _(w):
        base = w * hop_blocks

        def block(i):
            return norm[pl.ds(pl.multiple_of((base + i) * ROWS, ROWS), ROWS), :]

        off_w = off_ref[w]
        for a in range(NSUB):
            for h in range(SUB // BLK):
                i = a * (SUB // BLK) + h
                first = block(i)
                if i * BLK < JIT:
                    first = jnp.where(lane + i * BLK < off_w, block(i + 2 * hop_blocks), first)
                second = block(i + hop_blocks)
                cosine = cosw[pl.ds(w, 1), i * BLK:(i + 1) * BLK]
                total, delta = first + second, first - second
                cols = slice(h * BLK, (h + 1) * BLK)
                at = pl.ds(pl.multiple_of((w * NSUB + a) * ROWS, ROWS), ROWS)
                e_hi[at, cols], e_lo[at, cols] = split(total - cosine * delta)
                o_hi[at, cols], o_lo[at, cols] = split(delta - cosine * total)

    hook(0)
    ye[...] = mm(e_hi[...], te_hi[...]) + mm(e_hi[...], te_lo[...]) + mm(e_lo[...], te_hi[...])
    hook(1)
    yo[...] = mm(o_hi[...], to_hi[...]) + mm(o_hi[...], to_lo[...]) + mm(o_lo[...], to_hi[...])

    hook(2)
    inverse = 1.0 / bin_ref[1:2, :].astype(F32)
    reals, imags = [], []
    for w in range(windows):
        parts = []
        for parity, y in ((0, ye), (1, yo)):
            real = imag = None
            for a in range(NSUB):
                at = (w * NSUB + a) * ROWS
                yr, yi = y[at:at + ROWS, :HB], y[at:at + ROWS, HB:]
                row = (parity * NSUB + a) * 2
                c, s = tw_ref[row:row + 1, :], tw_ref[row + 1:row + 2, :]
                r, m = yr * c + yi * s, yi * c - yr * s
                real, imag = (r, m) if real is None else (real + r, imag + m)
            parts.append((real, imag))
        real = jnp.concatenate([parts[0][0], parts[1][0]], axis=1)
        imag = jnp.concatenate([parts[0][1], parts[1][1]], axis=1)
        c, s = turn[0, w:w + 1, :], turn[1, w:w + 1, :]
        reals.append(real * c - imag * s)
        imags.append(real * s + imag * c)
    real, imag = jnp.concatenate(reals, axis=0), jnp.concatenate(imags, axis=0)
    mag_hi, mag_lo = split(jnp.sqrt(real * real + imag * imag + 1e-12))
    smooth = (mm(mag_hi, band_ref[...]) + mm(mag_lo, band_ref[...])) * inverse + EPS
    white = ((real / smooth).astype(BF), (imag / smooth).astype(BF))
    for part in range(2):
        for w in range(windows):
            at = (part * CW + w % CW) * NF
            store(w // CW, at, white[part][w * ROWS:(w + 1) * ROWS, :])


def spectra_kernel(padded, blocks, windows, x_ref, dead_ref, off_ref, *refs):
    out_ref = refs[9]

    def store(k, at, value):
        out_ref[k, :, at:at + NF] = value

    spectra_group(padded, blocks, windows, pl.program_id(0), pl.program_id(0) == 0, store, lambda stage: None,
                  x_ref, dead_ref, off_ref, *refs[:9], *refs[10:])


def spectra_consts():
    tables = [box_table(), taper_table(), *transform_tables(), twiddle_table(), band_table(), bin_table()]
    return [jnp.asarray(t) for t in tables]


def spectra_scratch(norm_blocks, windows):
    rows = windows * NSUB * ROWS
    return [
        pltpu.VMEM((norm_blocks * ROWS, BLK), F32),
        pltpu.VMEM((windows, HALF), F32),
        pltpu.VMEM((2, windows, NF), F32),
    ] + [pltpu.VMEM((rows, SUB), BF)] * 4 + [pltpu.VMEM((rows, NF), F32)] * 2


def spectra(samples_in, dead_mask, offsets, padded, samples, windows):
    channels, width = samples_in.shape
    blocks = (samples + (HOP + JIT if padded else 0)) // BLK
    norm_blocks = (samples + HOP + JIT) // BLK
    consts = spectra_consts()
    whole = [pl.BlockSpec(c.shape, lambda i: (0, 0)) for c in consts]
    return pl.pallas_call(
        functools.partial(spectra_kernel, padded, blocks, windows),
        grid=(channels // ROWS,),
        out_shape=jax.ShapeDtypeStruct((windows // CW, channels, CHUNK), BF),
        in_specs=[
            pl.BlockSpec((ROWS, width), lambda i: (i, 0)),
            pl.BlockSpec(memory_space=pltpu.SMEM),
            pl.BlockSpec(memory_space=pltpu.SMEM),
        ] + whole,
        out_specs=pl.BlockSpec((windows // CW, ROWS, CHUNK), lambda i: (0, i, 0)),
        scratch_shapes=spectra_scratch(norm_blocks, windows),
        compiler_params=pltpu.CompilerParams(vmem_limit_bytes=56 << 20),
        name="spectra",
    )(samples_in, dead_mask, offsets, *consts)


def lag_table():
    lags = np.arange(NLAG) - NLAG // 2
    angle = 2 * np.pi * ((lags[:, None] * (K0 + BINS)[None, :]) % L) / L
    return np.stack([np.cos(angle), np.sin(angle)]).astype(np.float32)


GROUP = 8


def correlate_kernel(scale, devices, produce, own_ref, lag_ref, out_ref, feats, rot, total, send, recv):
    _, chunks, channels, _ = feats.shape
    per = chunks // 2
    groups = channels // ROWS
    units = 2 * groups
    lags = out_ref.shape[0]
    i = lax.axis_index("chan")
    r = lax.rem(i, 4)
    x, c = r // 2, lax.rem(r, 2)
    has_prev, has_next, has_third = i >= 4, i + 4 < devices, i + 8 < devices
    prev, following = i - 4, i + 4
    across, partner = i + 2 - 4 * x, i + 1 - 2 * c

    barrier = pltpu.get_barrier_semaphore()

    def greet(device):
        pl.semaphore_signal(barrier, inc=1, device_id={"chan": device}, device_id_type=MESH)

    greet(across)
    greet(partner)
    pl.when(has_prev)(lambda: greet(prev))
    pl.when(has_next)(lambda: greet(following))

    def all_here():
        pl.semaphore_wait(barrier, 2 + has_prev.astype(jnp.int32) + has_next.astype(jnp.int32))

    def unit(slot, k):
        return feats.at[slot, pl.ds(k % 2 * per, per), pl.ds(k // 2 * ROWS, ROWS)]

    def copy(item, k, source, slot, device):
        return pltpu.make_async_remote_copy(
            src_ref=unit(source, k),
            dst_ref=unit(slot, k),
            send_sem=send.at[item, k],
            recv_sem=recv.at[slot, k],
            device_id={"chan": device},
            device_id_type=MESH,
        )

    def arrived(slot, k):
        pltpu.make_async_copy(unit(slot, k), unit(slot, k), recv.at[slot, k]).wait()

    def left(item, k):
        pltpu.make_async_copy(unit(0, k), unit(0, k), send.at[item, k]).wait()

    def send_own(k):
        pl.when(has_prev)(lambda: copy(0, k, 0, 4, prev).start())
        pl.when(x == 1)(lambda: copy(2, k, 0, 2, across).start())
        pl.when(c == 1)(lambda: copy(4, k, 0, 1, partner).start())

    def first_forward(k):
        @pl.when(has_next)
        def _():
            arrived(4, k)
            pl.when(has_prev)(lambda: copy(1, k, 4, 8, prev).start())
            copy(2 + x, k, 4, 2 + 4 * x, across).start()
            copy(4 + c, k, 4, 3 + 2 * c, partner).start()

    def first_relay(k):
        @pl.when(i + 2 < devices)
        def _():
            arrived(2, k)
            copy(6, k, 2, 1 + 2 * c, partner).start()

    def last_forward(k):
        @pl.when(has_third)
        def _():
            arrived(8, k)
            pl.when(x == 0)(lambda: copy(3, k, 8, 6, across).start())
            pl.when(c == 0)(lambda: copy(5, k, 8, 7, partner).start())

    def last_relay(k):
        @pl.when(i + 6 < devices)
        def _():
            arrived(6, k)
            copy(7, k, 6, 5 + 2 * c, partner).start()

    for slot in range(1, 9):
        @pl.when(i + slot >= devices)
        def _(slot=slot):
            feats[slot] = jnp.zeros(feats.shape[1:], BF)

    size = GROUP * channels
    row = lax.broadcasted_iota(jnp.int32, (size, size), 0)
    col = lax.broadcasted_iota(jnp.int32, (size, size), 1)
    within = lax.rem(row, channels)
    flip = (col == row - within + (channels - 1 - within)).astype(F32).astype(BF)

    def rotate(k):
        backward = mm(flip[:channels, :channels], feats[0, k])
        for w in range(CW):
            lo, hi = w * NF, (CW + w) * NF
            real, imag = backward[:, lo:lo + NF], backward[:, hi:hi + NF]

            @pl.loop(0, lags, unroll=4)
            def _(t):
                co, si = lag_ref[0, pl.ds(t, 1), :], lag_ref[1, pl.ds(t, 1), :]
                at = pl.ds(pl.multiple_of(t * channels, channels), channels)
                rot[k, at, lo:lo + NF] = (real * co - imag * si).astype(BF)
                rot[k, at, hi:hi + NF] = (real * si + imag * co).astype(BF)

    def multiply(k):
        products = lax.dot_general(
            rot[k], feats[:, k].reshape(9 * channels, CHUNK), (((1,), (1,)), ((), ())),
            preferred_element_type=F32)
        if k == 0:
            total[...] = products
        elif k < chunks - 1:
            total[...] += products
        else:
            total[...] = (total[...] + products) * scale

    def odd_arrived(k):
        for slot in (1, 3, 5, 7):
            pl.when(i + slot < devices)(lambda slot=slot: arrived(slot, k))

    if produce is None:
        all_here()
        for k in range(chunks):
            feats[0, k] = own_ref[k]
        for k in range(units):
            send_own(k)
        early = 0
    else:
        def stages(stage):
            if stage < 2:
                first_forward(stage)
            else:
                first_relay(0)
                first_relay(1)

        produce(0, lambda stage: None)
        all_here()
        send_own(0)
        send_own(1)
        for group in range(1, groups):
            produce(group, stages if group == 1 else lambda stage: None)
            send_own(2 * group)
            send_own(2 * group + 1)
        early = 2
    turns = iter(range(chunks))

    def turn_some(count):
        for _ in range(count):
            k = next(turns, None)
            if k is not None:
                rotate(k)

    for k in range(early):
        last_forward(k)
    for k in range(early):
        last_relay(k)
    share = -(-chunks // max(1, units - early))
    for k in range(early, units):
        turn_some(share)
        first_forward(k)
    turn_some(chunks)
    for k in range(early, units):
        first_relay(k)
    for k in range(early):
        odd_arrived(k)
    for k in range(early, units):
        last_forward(k)
        if k > early:
            last_relay(k - 1)
    last_relay(units - 1)
    for half in range(2):
        for group in range(groups):
            if 2 * group + half >= early:
                odd_arrived(2 * group + half)
        for k in range(half * per, (half + 1) * per):
            multiply(k)

    cols = total.shape[1]
    wide = -(-cols // 128) * 128

    @pl.loop(0, lags // GROUP)
    def _(g):
        pieces = []
        for t in range(GROUP):
            at = pl.multiple_of((g * GROUP + t) * channels, channels)
            piece = total[pl.ds(at, channels), :]
            piece = jnp.concatenate([piece, jnp.zeros((channels, wide - cols), F32)], axis=1)
            piece = pltpu.roll(piece, wide - channels, 1, stride=1, stride_axis=0)
            pieces.append(piece[:, :NPART].astype(BF))
        result = mm(flip, jnp.concatenate(pieces, axis=0)).astype(BF)
        for t in range(GROUP):
            out_ref[g * GROUP + t] = result[t * channels:(t + 1) * channels, :]

    for k in range(units):
        pl.when(has_prev)(lambda k=k: left(0, k))
        pl.when(has_prev & has_next)(lambda k=k: left(1, k))
        for item, source in ((2, 4 - 4 * x), (3, 8 - 4 * x), (4, 4 - 4 * c), (5, 8 - 4 * c), (6, 2), (7, 6)):
            pl.when(i + source < devices)(lambda item=item, k=k: left(item, k))


def correlate_call(kernel, operands, specs, count, channels, chunks, extra):
    units = 2 * (channels // ROWS)
    return pl.pallas_call(
        kernel,
        out_shape=jax.ShapeDtypeStruct((count, channels, NPART), BF),
        in_specs=specs,
        out_specs=pl.BlockSpec(memory_space=pltpu.VMEM),
        scratch_shapes=[
            pltpu.VMEM((9, chunks, channels, CHUNK), BF),
            pltpu.VMEM((chunks, count * channels, CHUNK), BF),
            pltpu.VMEM((count * channels, 9 * channels), F32),
            pltpu.SemaphoreType.DMA((8, units)),
            pltpu.SemaphoreType.DMA((9, units)),
        ] + extra,
        compiler_params=pltpu.CompilerParams(
            collective_id=0, has_side_effects=True, vmem_limit_bytes=56 << 20),
        name="correlate",
    )(*operands)


def scale_of(chunks):
    return 1.0 / math.sqrt(2.0 * NF * chunks * CW)


def correlate(own, lags, devices):
    chunks, channels, _ = own.shape
    kernel = functools.partial(correlate_kernel, scale_of(chunks), devices, None)
    specs = [pl.BlockSpec(memory_space=pltpu.VMEM)] * 2
    return correlate_call(kernel, (own, lags), specs, lags.shape[1], channels, chunks, [])


def prepare_windows(windows, off_ref, taper_ref, bin_ref, cosw, turn):
    for w in range(windows):
        angle = jnp.full((8, 1), off_ref[w], jnp.int32).astype(F32) * (2.0 * math.pi / L)
        at = slice(8 * w, 8 * w + 8)
        cosw[at, :] = taper_ref[0:1, :] * jnp.cos(angle) + taper_ref[1:2, :] * jnp.sin(angle)
        turns = ((off_ref[w] * bin_ref[0:1, :]) & (L - 1)).astype(F32) * (2.0 * math.pi / L)
        turn[0, at, :] = jnp.broadcast_to(jnp.cos(turns), (8, NF))
        turn[1, at, :] = jnp.broadcast_to(jnp.sin(turns), (8, NF))


def repeat_rows(value, rows):
    return jnp.concatenate([value] * (rows // value.shape[0]), axis=0)


def normalise_window(w, box_ref, held, mags, norm):
    channels = held.shape[0]
    hop_blocks = HOP // BLK
    base = pl.multiple_of(w * HOP, HOP)

    def cols(first, count):
        return pl.ds(pl.multiple_of(base + first, 128), count)

    mags[:, cols(0, HOP)] = jnp.abs(held[:, cols(0, HOP)]).astype(BF)
    pieces = [mags[:, cols(b * BLK, BLK + 2 * H)] for b in range(hop_blocks)]
    level = mm(jnp.concatenate(pieces, axis=0), box_ref[...]) * (1.0 / (2 * H + 1)) + EPS
    values = jnp.concatenate([held[:, cols(H + b * BLK, BLK)] for b in range(hop_blocks)], axis=0)
    rows = hop_blocks * channels
    norm[pl.ds(pl.multiple_of(w * rows, rows), rows), :] = values / level


def fold_window(w, off_ref, norm, cosw, e_hi, e_lo, o_hi, o_lo):
    channels = e_hi.shape[0] // NSUB
    hop_blocks = HOP // BLK

    def block(i):
        return norm[pl.ds(pl.multiple_of((w * hop_blocks + i) * channels, channels), channels), :]

    lane = lax.broadcasted_iota(jnp.int32, (channels, BLK), 1)
    off_w = off_ref[w]
    per_w = pl.ds(pl.multiple_of(8 * w, 8), 8)
    for a in range(NSUB):
        for h in range(SUB // BLK):
            i = a * (SUB // BLK) + h
            first = block(i)
            if i * BLK < JIT:
                first = jnp.where(lane + i * BLK < off_w, block(i + 2 * hop_blocks), first)
            second = block(i + hop_blocks)
            cosine = repeat_rows(cosw[per_w, i * BLK:(i + 1) * BLK], channels)
            total, delta = first + second, first - second
            at, span = slice(a * channels, (a + 1) * channels), slice(h * BLK, (h + 1) * BLK)
            e_hi[at, span], e_lo[at, span] = split(total - cosine * delta)
            o_hi[at, span], o_lo[at, span] = split(delta - cosine * total)


def window_spectra(w, alive, te_hi, te_lo, to_hi, to_lo, tw_ref, band_ref, bin_ref, turn, e_hi, e_lo, o_hi, o_lo):
    channels = e_hi.shape[0] // NSUB
    per_w = pl.ds(pl.multiple_of(8 * w, 8), 8)
    parts = []
    for parity, (hi, lo, t_hi, t_lo) in enumerate(((e_hi, e_lo, te_hi, te_lo), (o_hi, o_lo, to_hi, to_lo))):
        y = mm(jnp.concatenate([hi[...], hi[...], lo[...]], axis=1),
               jnp.concatenate([t_hi[...], t_lo[...], t_hi[...]], axis=0))
        real = imag = None
        for a in range(NSUB):
            at = slice(a * channels, (a + 1) * channels)
            yr, yi = y[at, :HB], y[at, HB:]
            row = (parity * NSUB + a) * 2
            c, s = tw_ref[row:row + 1, :], tw_ref[row + 1:row + 2, :]
            r, m = yr * c + yi * s, yi * c - yr * s
            real, imag = (r, m) if real is None else (real + r, imag + m)
        parts.append((real, imag))
    real = jnp.concatenate([parts[0][0], parts[1][0]], axis=1)
    imag = jnp.concatenate([parts[0][1], parts[1][1]], axis=1)
    c, s = repeat_rows(turn[0, per_w, :], channels), repeat_rows(turn[1, per_w, :], channels)
    real, imag = real * c - imag * s, real * s + imag * c
    mag_hi, mag_lo = split(jnp.sqrt(real * real + imag * imag + 1e-12))
    inverse = 1.0 / bin_ref[1:2, :].astype(F32)
    smooth = (mm(mag_hi, band_ref[...]) + mm(mag_lo, band_ref[...])) * inverse + EPS
    return (real / smooth * alive).astype(BF), (imag / smooth * alive).astype(BF)


def flip_matrix(size, channels):
    row = lax.broadcasted_iota(jnp.int32, (size, size), 0)
    col = lax.broadcasted_iota(jnp.int32, (size, size), 1)
    within = lax.rem(row, channels)
    return (col == row - within + (channels - 1 - within)).astype(F32).astype(BF)


def align_kernel(scale, total, out_ref, staged, stored):
    lags, channels, _ = out_ref.shape
    size = GROUP * channels
    flip = flip_matrix(size, channels)
    far = 8 * channels

    def store(g):
        at = pl.ds(g * GROUP, GROUP)
        return pltpu.make_async_copy(staged.at[at], out_ref.at[at], stored.at[g])

    turned = []
    for g in range(lags // GROUP):
        values = (total[:, g * size:(g + 1) * size] * scale).astype(BF)
        values = jnp.concatenate(
            [values[:far], jnp.zeros((128 - channels, size), BF), values[far:]], axis=0)
        turned.append(lax.dot_general(flip, values, (((1,), (1,)), ((), ())), preferred_element_type=F32))
    for g in range(lags // GROUP):
        pieces = []
        for t in range(GROUP):
            piece = pltpu.roll(turned[g][t * channels:(t + 1) * channels, :], 0, 1, stride=1, stride_axis=0)
            pieces.append(piece[:, :NPART].astype(BF))
        result = mm(flip, jnp.concatenate(pieces, axis=0)).astype(BF)
        for t in range(GROUP):
            staged[g * GROUP + t] = result[t * channels:(t + 1) * channels, :]
        store(g).start()
    for g in range(lags // GROUP):
        store(g).wait()


def whole_kernel(devices, windows, records, dead_ref, off_ref, box_ref, taper_ref, te_hi, te_lo, to_hi, to_lo,
                 tw_ref, band_ref, bin_ref, lag_ref, total, feats, rot, send, recv, held, loaded, mags, norm, cosw, turn, e_hi, e_lo, o_hi, o_lo):
    channels, samples = records.shape
    lags = lag_ref.shape[1]
    half = lags // 2
    i = lax.axis_index("chan")
    r = lax.rem(i, 4)
    x, c = r // 2, lax.rem(r, 2)
    has_prev, has_next, has_third = i >= 4, i + 4 < devices, i + 8 < devices
    prev, following = i - 4, i + 4
    across, partner = i + 2 - 4 * x, i + 1 - 2 * c

    def load(w):
        first = max(0, w * HOP - H)
        last = (w + 1) * HOP - H if w < windows - 1 else samples
        return pltpu.make_async_copy(
            records.at[:, pl.ds(first, last - first)], held.at[:, pl.ds(first + H, last - first)], loaded.at[w])

    for w in reversed(range(windows)):
        load(w).start()

    barrier = pltpu.get_barrier_semaphore()

    def greet(device):
        pl.semaphore_signal(barrier, inc=1, device_id={"chan": device}, device_id_type=MESH)

    greet(across)
    greet(partner)
    pl.when(has_prev)(lambda: greet(prev))
    pl.when(has_next)(lambda: greet(following))
    slant_out, slant_in = (x == 0) & has_prev, (x == 1) & has_next
    pl.when(slant_out)(lambda: greet(i - 2))
    pl.when(slant_in)(lambda: greet(i + 2))
    late = max(0, windows - 2)

    def all_here():
        others = sum(flag.astype(jnp.int32) for flag in (has_prev, has_next, slant_out, slant_in))
        pl.semaphore_wait(barrier, 2 + others)

    def copy(item, k, source, slot, device):
        return pltpu.make_async_remote_copy(
            src_ref=feats.at[source, k],
            dst_ref=feats.at[slot, k],
            send_sem=send.at[item, k],
            recv_sem=recv.at[slot, k],
            device_id={"chan": device},
            device_id_type=MESH,
        )

    def arrived(slot, k):
        pltpu.make_async_copy(feats.at[slot, k], feats.at[slot, k], recv.at[slot, k]).wait()

    def left(item, k):
        pltpu.make_async_copy(feats.at[0, k], feats.at[0, k], send.at[item, k]).wait()

    def send_own(k):
        pl.when(has_prev)(lambda: copy(0, k, 0, 4, prev).start())
        pl.when(x == 1)(lambda: copy(2, k, 0, 2, across).start())
        pl.when(c == 1)(lambda: copy(4, k, 0, 1, partner).start())

    def forward_next(k, here):
        @pl.when(here & has_next)
        def _():
            arrived(4, k)
            pl.when(has_prev)(lambda: copy(1, k, 4, 8, prev).start())
            pl.when(slant_out & (k >= late))(lambda: copy(8, k, 4, 6, i - 2).start())
            copy(2 + x, k, 4, 2 + 4 * x, across).start()
            copy(4 + c, k, 4, 3 + 2 * c, partner).start()

    def relay_near(k, here):
        @pl.when(here & (i + 2 < devices))
        def _():
            arrived(2, k)
            copy(6, k, 2, 1 + 2 * c, partner).start()

    def forward_third(k, here):
        @pl.when(here & has_third)
        def _():
            arrived(8, k)
            pl.when((x == 0) & (k < late))(lambda: copy(3, k, 8, 6, across).start())
            pl.when(c == 0)(lambda: copy(5, k, 8, 7, partner).start())

    def relay_far(k, here):
        @pl.when(here & (i + 6 < devices))
        def _():
            arrived(6, k)
            copy(7, k, 6, 5 + 2 * c, partner).start()

    def there(k):
        return (k >= 0) & (k < windows)

    def mid_tick(n):
        k = n - FIRST
        forward_next(k, there(k))
        relay_near(k, there(k) & (x == 0))
        k = n - THIRD
        relay_far(k, there(k) & (k < late) & (x == 1))

    def end_tick(n):
        k = n - SECOND
        forward_third(k, there(k))
        relay_near(k, there(k) & (x == 1))
        relay_far(k, there(k) & ((x == 0) | (k >= late)))

    for slot in range(1, 9):
        @pl.when(i + slot >= devices)
        def _(slot=slot):
            feats[slot] = jnp.zeros(feats.shape[1:], BF)

    def rotate(k):
        real, imag = feats[0, k, :, :NF].astype(F32), feats[0, k, :, NF:].astype(F32)

        def put(t, a, b):
            rot[k, t * channels:(t + 1) * channels, :NF] = a.astype(BF)
            rot[k, t * channels:(t + 1) * channels, NF:] = b.astype(BF)

        put(half, real, imag)
        for step in range(1, half + 1):
            t = half - step
            co, si = lag_ref[0, t:t + 1, :], lag_ref[1, t:t + 1, :]
            rc, rs, ic, js = real * co, real * si, imag * co, imag * si
            put(t, rc - js, rs + ic)
            if half + step < lags:
                put(half + step, rc + js, ic - rs)

    def side(ref, units):
        return jnp.concatenate([ref(k) for k in units], axis=1)

    def product(units):
        return lax.dot_general(
            side(lambda k: jnp.concatenate([feats[1:9, k].reshape(8 * channels, 2 * NF), feats[0, k]], axis=0), units),
            side(lambda k: rot[k], units), (((1,), (1,)), ((), ())), preferred_element_type=F32)

    def multiply(units):
        for k in units:
            for slot in (1, 3, 5, 7):
                pl.when(i + slot < devices)(lambda slot=slot, k=k: arrived(slot, k))
        products = product(units)
        if units[0] == 0:
            total[...] = products
        else:
            total[...] += products

    channel = lax.broadcasted_iota(jnp.int32, (channels, 1), 0)
    dead = jnp.zeros((channels, 1), jnp.int32)
    for j in range(channels):
        dead = jnp.where(channel == j, dead_ref[j], dead)
    alive = (1 - dead).astype(F32)
    prepare_windows(windows, off_ref, taper_ref, bin_ref, cosw, turn)
    held[:, :H] = jnp.zeros((channels, H), F32)
    held[:, samples + H:] = jnp.zeros((channels, H), F32)
    tail = samples // BLK * channels
    norm[tail:, :] = jnp.zeros((norm.shape[0] - tail, BLK), F32)
    load(windows - 1).wait()
    all_here()
    mags[:, samples:] = jnp.abs(held[:, samples:]).astype(BF)

    normalise_window(windows - 1, box_ref, held, mags, norm)

    @pl.loop(0, windows)
    def _(n):
        w = windows - 1 - n
        ahead = jnp.maximum(w - 1, 0)
        pl.when(w == 1)(lambda: load(0).wait())
        if windows > 2:
            pl.when(w > 1)(lambda: pltpu.make_async_copy(
                records.at[:, pl.ds(H, HOP)], held.at[:, pl.ds(H, HOP)], loaded.at[ahead]).wait())
        mid_tick(n)
        fold_window(w, off_ref, norm, cosw, e_hi, e_lo, o_hi, o_lo)
        normalise_window(ahead, box_ref, held, mags, norm)
        real, imag = window_spectra(
            w, alive, te_hi, te_lo, to_hi, to_lo, tw_ref, band_ref, bin_ref, turn, e_hi, e_lo, o_hi, o_lo)
        feats[0, n, :, :NF] = real
        feats[0, n, :, NF:] = imag
        send_own(n)
        end_tick(n)
        rotate(n)

    pairs = [range(k, k + 2) for k in range(0, windows, 2)]
    early = [[k for pair in pairs[:-2] for k in pair], pairs[-2], pairs[-1][:1]]
    def hook_of(units):
        return max([2 * (k + SECOND) + 1 for k in units] + [2 * (k + THIRD) for k in units if k < late])

    tasks = []
    tasks += [(hook_of(units), lambda u=units: multiply(u)) for units in early]
    for hook in range(2 * windows, 2 * max(windows + SECOND, late + THIRD)):
        (end_tick if hook % 2 else mid_tick)(hook // 2)
        if tasks and tasks[0][0] <= hook:
            tasks.pop(0)[1]()
    for _, task in tasks:
        task()
    multiply(pairs[-1][1:])

    @pl.loop(0, windows)
    def _(k):
        pl.when(has_prev)(lambda: left(0, k))
        pl.when(has_prev & has_next)(lambda: left(1, k))
        pl.when((i + 4 - 4 * x < devices))(lambda: left(2, k))
        pl.when(jnp.where(x == 1, has_next, has_third & (k < late)))(lambda: left(3, k))
        for item, source in ((4, 4 - 4 * c), (5, 8 - 4 * c), (6, 2), (7, 6)):
            pl.when(i + source < devices)(lambda item=item: left(item, k))
        pl.when(slant_out & has_next & (k >= late))(lambda: left(8, k))


def whole(records, dead_mask, offsets, lags, devices):
    channels, samples = records.shape
    windows = samples // HOP
    count = lags.shape[1]
    consts = spectra_consts()
    vmem, smem = pl.BlockSpec(memory_space=pltpu.VMEM), pl.BlockSpec(memory_space=pltpu.SMEM)
    rows = NSUB * channels
    total = pl.pallas_call(
        functools.partial(whole_kernel, devices, windows),
        out_shape=pltpu.VMEM((9 * channels, count * channels), F32),
        in_specs=[pl.BlockSpec(memory_space=pl.ANY), smem, smem] + [vmem] * (len(consts) + 1),
        out_specs=vmem,
        scratch_shapes=[
            pltpu.VMEM((9, windows, channels, 2 * NF), BF),
            pltpu.VMEM((windows, count * channels, 2 * NF), BF),
            pltpu.SemaphoreType.DMA((9, windows)),
            pltpu.SemaphoreType.DMA((9, windows)),
            pltpu.VMEM((channels, samples + 2 * H), F32),
            pltpu.SemaphoreType.DMA((windows,)),
            pltpu.VMEM((channels, samples + 2 * H), BF),
            pltpu.VMEM(((samples + HOP + JIT) // BLK * channels, BLK), F32),
            pltpu.VMEM((8 * windows, HALF), F32),
            pltpu.VMEM((2, 8 * windows, NF), F32),
        ] + [pltpu.VMEM((rows, SUB), BF)] * 4,
        compiler_params=pltpu.CompilerParams(
            collective_id=0, has_side_effects=True, vmem_limit_bytes=56 << 20),
        name="correlate",
    )(records, dead_mask, offsets, *consts, lags)
    return pl.pallas_call(
        functools.partial(align_kernel, 1.0 / math.sqrt(2.0 * NF * windows)),
        out_shape=jax.ShapeDtypeStruct((count, channels, NPART), BF),
        in_specs=[vmem],
        out_specs=pl.BlockSpec(memory_space=pl.ANY),
        scratch_shapes=[
            pltpu.VMEM((count, channels, NPART), BF),
            pltpu.SemaphoreType.DMA((count // GROUP,)),
        ],
        compiler_params=pltpu.CompilerParams(vmem_limit_bytes=8 << 20),
        name="align",
    )(total)


def shifted(value, axis, steps):
    count = lax.axis_size(axis)
    leading, last = (max(0, -steps), min(count, count - steps))
    return lax.ppermute(value, axis, [(source, source + steps) for source in range(leading, last)])


def local(records, dead_mask, offsets):
    channels, samples = records.shape
    tm_count = lax.axis_size("tm")
    tm_index = lax.axis_index("tm")
    windows = samples // HOP
    lags = jnp.asarray(lag_table())
    devices = lax.axis_size("chan")
    if tm_count == 1:
        return whole(records, dead_mask, offsets, lags, devices)
    left = shifted(records[:, -H:], "tm", 1)
    right = shifted(records[:, :HOP + JIT + H], "tm", -1)
    values = jnp.concatenate([left, records, right], axis=1)
    own_offsets = lax.dynamic_slice_in_dim(offsets, tm_index * windows, windows, 0)
    own = spectra(values, dead_mask, own_offsets, True, samples, windows)
    own = lax.all_gather(own, "tm", axis=0, tiled=True)
    lags_local = NLAG // tm_count
    lags = lax.dynamic_slice_in_dim(lags, tm_index * lags_local, lags_local, 1)
    return correlate(own, lags, devices)


def solution(mesh):
    return jax.shard_map(
        local,
        mesh=mesh,
        in_specs=(P(("win", "chan"), "tm"), P(("win", "chan")), P("win")),
        out_specs=P("tm", ("win", "chan"), None),
        check_vma=False,
    )
```

```python
import functools
import math

import jax
import jax.numpy as jnp
import numpy as np
from jax import lax
from jax.experimental import pallas as pl
from jax.experimental.pallas import tpu as pltpu
from jax.sharding import PartitionSpec as P

L = 8192
HOP = 4096
JIT = 512
H = 128
K0 = 32
NF = 256
WB = 64
NLAG = 32
NPART = 256

EPS = 1e-05
BLK = 256
SUB = 512
HALF = L // 2
NSUB = HALF // SUB
HB = NF // 2
ROWS = 16
CW = 2
CHUNK = 2 * CW * NF
MESH = pl.DeviceIdType.MESH
FIRST, SECOND, THIRD = 4, 6, 9
BF = jnp.bfloat16
F32 = jnp.float32

BINS = np.concatenate([np.arange(0, NF, 2), np.arange(1, NF, 2)])


def split_np(value):
    high = value.astype(jnp.bfloat16)
    low = (value - high.astype(np.float64)).astype(jnp.bfloat16)
    return high, low


def transform_tables():
    tables = []
    for parity in range(2):
        k = K0 + np.arange(parity, NF, 2)
        angle = 2 * np.pi * ((np.arange(SUB)[:, None] * k[None, :]) % L) / L
        tables.extend(split_np(np.concatenate([np.cos(angle), -np.sin(angle)], axis=1)))
    return tables


def twiddle_table():
    rows = []
    for parity in range(2):
        k = K0 + np.arange(parity, NF, 2)
        for a in range(NSUB):
            angle = 2 * np.pi * ((SUB * a * k) % L) / L
            rows.append(0.5 * np.cos(angle))
            rows.append(0.5 * np.sin(angle))
    return np.stack(rows).astype(np.float32)


def box_table():
    i = np.arange(BLK + 2 * H)[:, None]
    j = np.arange(BLK)[None, :] + H
    return (np.abs(i - j) <= H).astype(jnp.bfloat16)


def taper_table():
    angle = 2 * np.pi * np.arange(HALF) / L
    return np.stack([np.cos(angle), np.sin(angle)]).astype(np.float32)


def band_table():
    return (np.abs(BINS[:, None] - BINS[None, :]) <= WB).astype(jnp.bfloat16)


def bin_table():
    q = np.arange(NF)
    counts = (np.abs(q[:, None] - q[None, :]) <= WB).sum(axis=0)[BINS]
    return np.stack([K0 + BINS, counts]).astype(np.int32)


def split(value):
    high = value.astype(BF)
    return high, (value - high.astype(F32)).astype(BF)


def mm(a, b):
    return jnp.dot(a, b, preferred_element_type=F32)


def spectra_group(padded, blocks, windows, group, prepare, store, hook, x_ref, dead_ref, off_ref, box_ref,
                  taper_ref, te_hi, te_lo, to_hi, to_lo, tw_ref, band_ref, bin_ref, norm, cosw, turn, e_hi,
                  e_lo, o_hi, o_lo, ye, yo):
    tail = norm.shape[0] - blocks * ROWS

    @pl.when(prepare)
    def _():
        window = lax.broadcasted_iota(jnp.int32, (windows, 1), 0)
        off = jnp.zeros((windows, 1), jnp.int32)
        for w in range(windows):
            off = jnp.where(window == w, off_ref[w], off)
        angle = off.astype(F32) * (2.0 * math.pi / L)
        cosw[...] = taper_ref[0:1, :] * jnp.cos(angle) + taper_ref[1:2, :] * jnp.sin(angle)
        turns = ((off * bin_ref[0:1, :]) & (L - 1)).astype(F32) * (2.0 * math.pi / L)
        turn[0] = jnp.cos(turns)
        turn[1] = jnp.sin(turns)
        if tail:
            norm[blocks * ROWS:, :] = jnp.zeros((tail, BLK), F32)

    channel = lax.broadcasted_iota(jnp.int32, (ROWS, 1), 0)
    dead = jnp.zeros((ROWS, 1), jnp.int32)
    for c in range(ROWS):
        dead = jnp.where(channel == c, dead_ref[group * ROWS + c], dead)
    alive = (1 - dead).astype(F32)
    per = 16
    shift = H if padded else 0

    def normalise(first, count, left_edge, right_edge):
        mags, vals = [], []
        for i in range(count):
            base = (first + i) * BLK + shift
            at = base if isinstance(base, int) else pl.multiple_of(base, 128)
            vals.append(x_ref[:, pl.ds(at, BLK)] * alive)
            pieces = []
            lo = base - H if isinstance(base, int) else pl.multiple_of(base - H, 128)
            if left_edge and i == 0:
                pieces = [jnp.zeros((ROWS, H), F32), x_ref[:, pl.ds(at, BLK + H)]]
            elif right_edge and i == count - 1:
                pieces = [x_ref[:, pl.ds(lo, BLK + H)], jnp.zeros((ROWS, H), F32)]
            else:
                pieces = [x_ref[:, pl.ds(lo, BLK + 2 * H)]]
            piece = pieces[0] if len(pieces) == 1 else jnp.concatenate(pieces, axis=1)
            mags.append(jnp.abs(piece * alive).astype(BF))
        level = mm(jnp.concatenate(mags, axis=0), box_ref[...]) * (1.0 / (2 * H + 1))
        value = jnp.concatenate(vals, axis=0) / (level + EPS)
        at = first * ROWS if isinstance(first, int) else pl.multiple_of(first * ROWS, ROWS)
        norm[pl.ds(at, count * ROWS), :] = value

    if padded:
        full = blocks // per

        @pl.loop(0, full)
        def _(i):
            normalise(i * per, per, False, False)

        if blocks % per:
            normalise(full * per, blocks % per, False, False)
    else:
        normalise(0, per, True, blocks == per)

        @pl.loop(1, blocks // per - 1)
        def _(i):
            normalise(i * per, per, False, False)

        if blocks > per:
            normalise(blocks - per, per, False, True)

    lane = lax.broadcasted_iota(jnp.int32, (ROWS, BLK), 1)
    hop_blocks = HOP // BLK

    @pl.loop(0, windows)
    def _(w):
        base = w * hop_blocks

        def block(i):
            return norm[pl.ds(pl.multiple_of((base + i) * ROWS, ROWS), ROWS), :]

        off_w = off_ref[w]
        for a in range(NSUB):
            for h in range(SUB // BLK):
                i = a * (SUB // BLK) + h
                first = block(i)
                if i * BLK < JIT:
                    first = jnp.where(lane + i * BLK < off_w, block(i + 2 * hop_blocks), first)
                second = block(i + hop_blocks)
                cosine = cosw[pl.ds(w, 1), i * BLK:(i + 1) * BLK]
                total, delta = first + second, first - second
                cols = slice(h * BLK, (h + 1) * BLK)
                at = pl.ds(pl.multiple_of((w * NSUB + a) * ROWS, ROWS), ROWS)
                e_hi[at, cols], e_lo[at, cols] = split(total - cosine * delta)
                o_hi[at, cols], o_lo[at, cols] = split(delta - cosine * total)

    hook(0)
    ye[...] = mm(e_hi[...], te_hi[...]) + mm(e_hi[...], te_lo[...]) + mm(e_lo[...], te_hi[...])
    hook(1)
    yo[...] = mm(o_hi[...], to_hi[...]) + mm(o_hi[...], to_lo[...]) + mm(o_lo[...], to_hi[...])

    hook(2)
    inverse = 1.0 / bin_ref[1:2, :].astype(F32)
    reals, imags = [], []
    for w in range(windows):
        parts = []
        for parity, y in ((0, ye), (1, yo)):
            real = imag = None
            for a in range(NSUB):
                at = (w * NSUB + a) * ROWS
                yr, yi = y[at:at + ROWS, :HB], y[at:at + ROWS, HB:]
                row = (parity * NSUB + a) * 2
                c, s = tw_ref[row:row + 1, :], tw_ref[row + 1:row + 2, :]
                r, m = yr * c + yi * s, yi * c - yr * s
                real, imag = (r, m) if real is None else (real + r, imag + m)
            parts.append((real, imag))
        real = jnp.concatenate([parts[0][0], parts[1][0]], axis=1)
        imag = jnp.concatenate([parts[0][1], parts[1][1]], axis=1)
        c, s = turn[0, w:w + 1, :], turn[1, w:w + 1, :]
        reals.append(real * c - imag * s)
        imags.append(real * s + imag * c)
    real, imag = jnp.concatenate(reals, axis=0), jnp.concatenate(imags, axis=0)
    mag_hi, mag_lo = split(jnp.sqrt(real * real + imag * imag + 1e-12))
    smooth = (mm(mag_hi, band_ref[...]) + mm(mag_lo, band_ref[...])) * inverse + EPS
    white = ((real / smooth).astype(BF), (imag / smooth).astype(BF))
    for part in range(2):
        for w in range(windows):
            at = (part * CW + w % CW) * NF
            store(w // CW, at, white[part][w * ROWS:(w + 1) * ROWS, :])


def spectra_kernel(padded, blocks, windows, x_ref, dead_ref, off_ref, *refs):
    out_ref = refs[9]

    def store(k, at, value):
        out_ref[k, :, at:at + NF] = value

    spectra_group(padded, blocks, windows, pl.program_id(0), pl.program_id(0) == 0, store, lambda stage: None,
                  x_ref, dead_ref, off_ref, *refs[:9], *refs[10:])


def spectra_consts():
    tables = [box_table(), taper_table(), *transform_tables(), twiddle_table(), band_table(), bin_table()]
    return [jnp.asarray(t) for t in tables]


def spectra_scratch(norm_blocks, windows):
    rows = windows * NSUB * ROWS
    return [
        pltpu.VMEM((norm_blocks * ROWS, BLK), F32),
        pltpu.VMEM((windows, HALF), F32),
        pltpu.VMEM((2, windows, NF), F32),
    ] + [pltpu.VMEM((rows, SUB), BF)] * 4 + [pltpu.VMEM((rows, NF), F32)] * 2


def spectra(samples_in, dead_mask, offsets, padded, samples, windows):
    channels, width = samples_in.shape
    blocks = (samples + (HOP + JIT if padded else 0)) // BLK
    norm_blocks = (samples + HOP + JIT) // BLK
    consts = spectra_consts()
    whole = [pl.BlockSpec(c.shape, lambda i: (0, 0)) for c in consts]
    return pl.pallas_call(
        functools.partial(spectra_kernel, padded, blocks, windows),
        grid=(channels // ROWS,),
        out_shape=jax.ShapeDtypeStruct((windows // CW, channels, CHUNK), BF),
        in_specs=[
            pl.BlockSpec((ROWS, width), lambda i: (i, 0)),
            pl.BlockSpec(memory_space=pltpu.SMEM),
            pl.BlockSpec(memory_space=pltpu.SMEM),
        ] + whole,
        out_specs=pl.BlockSpec((windows // CW, ROWS, CHUNK), lambda i: (0, i, 0)),
        scratch_shapes=spectra_scratch(norm_blocks, windows),
        compiler_params=pltpu.CompilerParams(vmem_limit_bytes=56 << 20),
        name="spectra",
    )(samples_in, dead_mask, offsets, *consts)


def lag_table():
    lags = np.arange(NLAG) - NLAG // 2
    angle = 2 * np.pi * ((lags[:, None] * (K0 + BINS)[None, :]) % L) / L
    return np.stack([np.cos(angle), np.sin(angle)]).astype(np.float32)


GROUP = 8


def correlate_kernel(scale, devices, produce, own_ref, lag_ref, out_ref, feats, rot, total, send, recv):
    _, chunks, channels, _ = feats.shape
    per = chunks // 2
    groups = channels // ROWS
    units = 2 * groups
    lags = out_ref.shape[0]
    i = lax.axis_index("chan")
    r = lax.rem(i, 4)
    x, c = r // 2, lax.rem(r, 2)
    has_prev, has_next, has_third = i >= 4, i + 4 < devices, i + 8 < devices
    prev, following = i - 4, i + 4
    across, partner = i + 2 - 4 * x, i + 1 - 2 * c

    barrier = pltpu.get_barrier_semaphore()

    def greet(device):
        pl.semaphore_signal(barrier, inc=1, device_id={"chan": device}, device_id_type=MESH)

    greet(across)
    greet(partner)
    pl.when(has_prev)(lambda: greet(prev))
    pl.when(has_next)(lambda: greet(following))

    def all_here():
        pl.semaphore_wait(barrier, 2 + has_prev.astype(jnp.int32) + has_next.astype(jnp.int32))

    def unit(slot, k):
        return feats.at[slot, pl.ds(k % 2 * per, per), pl.ds(k // 2 * ROWS, ROWS)]

    def copy(item, k, source, slot, device):
        return pltpu.make_async_remote_copy(
            src_ref=unit(source, k),
            dst_ref=unit(slot, k),
            send_sem=send.at[item, k],
            recv_sem=recv.at[slot, k],
            device_id={"chan": device},
            device_id_type=MESH,
        )

    def arrived(slot, k):
        pltpu.make_async_copy(unit(slot, k), unit(slot, k), recv.at[slot, k]).wait()

    def left(item, k):
        pltpu.make_async_copy(unit(0, k), unit(0, k), send.at[item, k]).wait()

    def send_own(k):
        pl.when(has_prev)(lambda: copy(0, k, 0, 4, prev).start())
        pl.when(x == 1)(lambda: copy(2, k, 0, 2, across).start())
        pl.when(c == 1)(lambda: copy(4, k, 0, 1, partner).start())

    def first_forward(k):
        @pl.when(has_next)
        def _():
            arrived(4, k)
            pl.when(has_prev)(lambda: copy(1, k, 4, 8, prev).start())
            copy(2 + x, k, 4, 2 + 4 * x, across).start()
            copy(4 + c, k, 4, 3 + 2 * c, partner).start()

    def first_relay(k):
        @pl.when(i + 2 < devices)
        def _():
            arrived(2, k)
            copy(6, k, 2, 1 + 2 * c, partner).start()

    def last_forward(k):
        @pl.when(has_third)
        def _():
            arrived(8, k)
            pl.when(x == 0)(lambda: copy(3, k, 8, 6, across).start())
            pl.when(c == 0)(lambda: copy(5, k, 8, 7, partner).start())

    def last_relay(k):
        @pl.when(i + 6 < devices)
        def _():
            arrived(6, k)
            copy(7, k, 6, 5 + 2 * c, partner).start()

    for slot in range(1, 9):
        @pl.when(i + slot >= devices)
        def _(slot=slot):
            feats[slot] = jnp.zeros(feats.shape[1:], BF)

    size = GROUP * channels
    row = lax.broadcasted_iota(jnp.int32, (size, size), 0)
    col = lax.broadcasted_iota(jnp.int32, (size, size), 1)
    within = lax.rem(row, channels)
    flip = (col == row - within + (channels - 1 - within)).astype(F32).astype(BF)

    def rotate(k):
        backward = mm(flip[:channels, :channels], feats[0, k])
        for w in range(CW):
            lo, hi = w * NF, (CW + w) * NF
            real, imag = backward[:, lo:lo + NF], backward[:, hi:hi + NF]

            @pl.loop(0, lags, unroll=4)
            def _(t):
                co, si = lag_ref[0, pl.ds(t, 1), :], lag_ref[1, pl.ds(t, 1), :]
                at = pl.ds(pl.multiple_of(t * channels, channels), channels)
                rot[k, at, lo:lo + NF] = (real * co - imag * si).astype(BF)
                rot[k, at, hi:hi + NF] = (real * si + imag * co).astype(BF)

    def multiply(k):
        products = lax.dot_general(
            rot[k], feats[:, k].reshape(9 * channels, CHUNK), (((1,), (1,)), ((), ())),
            preferred_element_type=F32)
        if k == 0:
            total[...] = products
        elif k < chunks - 1:
            total[...] += products
        else:
            total[...] = (total[...] + products) * scale

    def odd_arrived(k):
        for slot in (1, 3, 5, 7):
            pl.when(i + slot < devices)(lambda slot=slot: arrived(slot, k))

    if produce is None:
        all_here()
        for k in range(chunks):
            feats[0, k] = own_ref[k]
        for k in range(units):
            send_own(k)
        early = 0
    else:
        def stages(stage):
            if stage < 2:
                first_forward(stage)
            else:
                first_relay(0)
                first_relay(1)

        produce(0, lambda stage: None)
        all_here()
        send_own(0)
        send_own(1)
        for group in range(1, groups):
            produce(group, stages if group == 1 else lambda stage: None)
            send_own(2 * group)
            send_own(2 * group + 1)
        early = 2
    turns = iter(range(chunks))

    def turn_some(count):
        for _ in range(count):
            k = next(turns, None)
            if k is not None:
                rotate(k)

    for k in range(early):
        last_forward(k)
    for k in range(early):
        last_relay(k)
    share = -(-chunks // max(1, units - early))
    for k in range(early, units):
        turn_some(share)
        first_forward(k)
    turn_some(chunks)
    for k in range(early, units):
        first_relay(k)
    for k in range(early):
        odd_arrived(k)
    for k in range(early, units):
        last_forward(k)
        if k > early:
            last_relay(k - 1)
    last_relay(units - 1)
    for half in range(2):
        for group in range(groups):
            if 2 * group + half >= early:
                odd_arrived(2 * group + half)
        for k in range(half * per, (half + 1) * per):
            multiply(k)

    cols = total.shape[1]
    wide = -(-cols // 128) * 128

    @pl.loop(0, lags // GROUP)
    def _(g):
        pieces = []
        for t in range(GROUP):
            at = pl.multiple_of((g * GROUP + t) * channels, channels)
            piece = total[pl.ds(at, channels), :]
            piece = jnp.concatenate([piece, jnp.zeros((channels, wide - cols), F32)], axis=1)
            piece = pltpu.roll(piece, wide - channels, 1, stride=1, stride_axis=0)
            pieces.append(piece[:, :NPART].astype(BF))
        result = mm(flip, jnp.concatenate(pieces, axis=0)).astype(BF)
        for t in range(GROUP):
            out_ref[g * GROUP + t] = result[t * channels:(t + 1) * channels, :]

    for k in range(units):
        pl.when(has_prev)(lambda k=k: left(0, k))
        pl.when(has_prev & has_next)(lambda k=k: left(1, k))
        for item, source in ((2, 4 - 4 * x), (3, 8 - 4 * x), (4, 4 - 4 * c), (5, 8 - 4 * c), (6, 2), (7, 6)):
            pl.when(i + source < devices)(lambda item=item, k=k: left(item, k))


def correlate_call(kernel, operands, specs, count, channels, chunks, extra):
    units = 2 * (channels // ROWS)
    return pl.pallas_call(
        kernel,
        out_shape=jax.ShapeDtypeStruct((count, channels, NPART), BF),
        in_specs=specs,
        out_specs=pl.BlockSpec(memory_space=pltpu.VMEM),
        scratch_shapes=[
            pltpu.VMEM((9, chunks, channels, CHUNK), BF),
            pltpu.VMEM((chunks, count * channels, CHUNK), BF),
            pltpu.VMEM((count * channels, 9 * channels), F32),
            pltpu.SemaphoreType.DMA((8, units)),
            pltpu.SemaphoreType.DMA((9, units)),
        ] + extra,
        compiler_params=pltpu.CompilerParams(
            collective_id=0, has_side_effects=True, vmem_limit_bytes=56 << 20),
        name="correlate",
    )(*operands)


def scale_of(chunks):
    return 1.0 / math.sqrt(2.0 * NF * chunks * CW)


def correlate(own, lags, devices):
    chunks, channels, _ = own.shape
    kernel = functools.partial(correlate_kernel, scale_of(chunks), devices, None)
    specs = [pl.BlockSpec(memory_space=pltpu.VMEM)] * 2
    return correlate_call(kernel, (own, lags), specs, lags.shape[1], channels, chunks, [])


def prepare_windows(windows, off_ref, taper_ref, bin_ref, cosw, turn):
    for w in range(windows):
        angle = jnp.full((8, 1), off_ref[w], jnp.int32).astype(F32) * (2.0 * math.pi / L)
        at = slice(8 * w, 8 * w + 8)
        cosw[at, :] = taper_ref[0:1, :] * jnp.cos(angle) + taper_ref[1:2, :] * jnp.sin(angle)
        turns = ((off_ref[w] * bin_ref[0:1, :]) & (L - 1)).astype(F32) * (2.0 * math.pi / L)
        turn[0, at, :] = jnp.broadcast_to(jnp.cos(turns), (8, NF))
        turn[1, at, :] = jnp.broadcast_to(jnp.sin(turns), (8, NF))


def repeat_rows(value, rows):
    return jnp.concatenate([value] * (rows // value.shape[0]), axis=0)


def normalise_window(w, box_ref, held, mags, norm):
    channels = held.shape[0]
    hop_blocks = HOP // BLK
    base = pl.multiple_of(w * HOP, HOP)

    def cols(first, count):
        return pl.ds(pl.multiple_of(base + first, 128), count)

    mags[:, cols(0, HOP)] = jnp.abs(held[:, cols(0, HOP)]).astype(BF)
    pieces = [mags[:, cols(b * BLK, BLK + 2 * H)] for b in range(hop_blocks)]
    level = mm(jnp.concatenate(pieces, axis=0), box_ref[...]) * (1.0 / (2 * H + 1)) + EPS
    values = jnp.concatenate([held[:, cols(H + b * BLK, BLK)] for b in range(hop_blocks)], axis=0)
    rows = hop_blocks * channels
    norm[pl.ds(pl.multiple_of(w * rows, rows), rows), :] = values / level


def fold_window(w, off_ref, norm, cosw, e_hi, e_lo, o_hi, o_lo):
    channels = e_hi.shape[0] // NSUB
    hop_blocks = HOP // BLK

    def block(i):
        return norm[pl.ds(pl.multiple_of((w * hop_blocks + i) * channels, channels), channels), :]

    lane = lax.broadcasted_iota(jnp.int32, (channels, BLK), 1)
    off_w = off_ref[w]
    per_w = pl.ds(pl.multiple_of(8 * w, 8), 8)
    for a in range(NSUB):
        for h in range(SUB // BLK):
            i = a * (SUB // BLK) + h
            first = block(i)
            if i * BLK < JIT:
                first = jnp.where(lane + i * BLK < off_w, block(i + 2 * hop_blocks), first)
            second = block(i + hop_blocks)
            cosine = repeat_rows(cosw[per_w, i * BLK:(i + 1) * BLK], channels)
            total, delta = first + second, first - second
            at, span = slice(a * channels, (a + 1) * channels), slice(h * BLK, (h + 1) * BLK)
            e_hi[at, span], e_lo[at, span] = split(total - cosine * delta)
            o_hi[at, span], o_lo[at, span] = split(delta - cosine * total)


def transform(folded, t_hi, t_lo, tw_ref, parity):
    hi, lo = folded
    channels = hi.shape[0] // NSUB
    y = mm(jnp.concatenate([hi[...], hi[...], lo[...]], axis=1),
           jnp.concatenate([t_hi[...], t_lo[...], t_hi[...]], axis=0))
    real = imag = None
    for a in range(NSUB):
        at = slice(a * channels, (a + 1) * channels)
        yr, yi = y[at, :HB], y[at, HB:]
        row = (parity * NSUB + a) * 2
        c, s = tw_ref[row:row + 1, :], tw_ref[row + 1:row + 2, :]
        r, m = yr * c + yi * s, yi * c - yr * s
        real, imag = (r, m) if real is None else (real + r, imag + m)
    return real, imag


def whiten(w, parts, alive, band_ref, bin_ref, turn):
    channels = alive.shape[0]
    per_w = pl.ds(pl.multiple_of(8 * w, 8), 8)
    real = jnp.concatenate([parts[0][0], parts[1][0]], axis=1)
    imag = jnp.concatenate([parts[0][1], parts[1][1]], axis=1)
    c, s = repeat_rows(turn[0, per_w, :], channels), repeat_rows(turn[1, per_w, :], channels)
    real, imag = real * c - imag * s, real * s + imag * c
    mag_hi, mag_lo = split(jnp.sqrt(real * real + imag * imag + 1e-12))
    inverse = 1.0 / bin_ref[1:2, :].astype(F32)
    smooth = (mm(mag_hi, band_ref[...]) + mm(mag_lo, band_ref[...])) * inverse + EPS
    return (real / smooth * alive).astype(BF), (imag / smooth * alive).astype(BF)


def flip_matrix(size, channels):
    row = lax.broadcasted_iota(jnp.int32, (size, size), 0)
    col = lax.broadcasted_iota(jnp.int32, (size, size), 1)
    within = lax.rem(row, channels)
    return (col == row - within + (channels - 1 - within)).astype(F32).astype(BF)


def align_kernel(scale, total, out_ref, staged, stored):
    lags, channels, _ = out_ref.shape
    size = GROUP * channels
    flip = flip_matrix(size, channels)
    far = 8 * channels

    def store(g):
        at = pl.ds(g * GROUP, GROUP)
        return pltpu.make_async_copy(staged.at[at], out_ref.at[at], stored.at[g])

    turned = []
    for g in range(lags // GROUP):
        values = (total[:, g * size:(g + 1) * size] * scale).astype(BF)
        values = jnp.concatenate(
            [values[:far], jnp.zeros((128 - channels, size), BF), values[far:]], axis=0)
        turned.append(lax.dot_general(flip, values, (((1,), (1,)), ((), ())), preferred_element_type=F32))
    for g in range(lags // GROUP):
        pieces = []
        for t in range(GROUP):
            piece = pltpu.roll(turned[g][t * channels:(t + 1) * channels, :], 0, 1, stride=1, stride_axis=0)
            pieces.append(piece[:, :NPART].astype(BF))
        result = mm(flip, jnp.concatenate(pieces, axis=0)).astype(BF)
        for t in range(GROUP):
            staged[g * GROUP + t] = result[t * channels:(t + 1) * channels, :]
        store(g).start()
    for g in range(lags // GROUP):
        store(g).wait()


def whole_kernel(devices, windows, records, dead_ref, off_ref, *refs):
    sources, total, refs = refs[:10], refs[10], refs[11:]
    feats, rot, send, recv, held, loaded, mags, norm, cosw, turn, *folded = refs[:18]
    tables, fetched = refs[18:28], refs[28]
    box_ref, taper_ref, te_hi, te_lo, to_hi, to_lo, tw_ref, band_ref, bin_ref, lag_ref = tables
    channels, samples = records.shape
    lags = lag_ref.shape[1]
    half = lags // 2
    i = lax.axis_index("chan")
    r = lax.rem(i, 4)
    x, c = r // 2, lax.rem(r, 2)
    has_prev, has_next, has_third = i >= 4, i + 4 < devices, i + 8 < devices
    prev, following = i - 4, i + 4
    across, partner = i + 2 - 4 * x, i + 1 - 2 * c

    def load(w):
        first = max(0, w * HOP - H)
        last = (w + 1) * HOP - H if w < windows - 1 else samples
        return pltpu.make_async_copy(
            records.at[:, pl.ds(first, last - first)], held.at[:, pl.ds(first + H, last - first)], loaded.at[w])

    def fetch(t):
        return pltpu.make_async_copy(sources[t], tables[t], fetched.at[t])

    first_tables, later_tables = (1, 8, 0), (2, 3, 4, 5, 6, 7, 9)

    barrier = pltpu.get_barrier_semaphore()

    def greet(device):
        pl.semaphore_signal(barrier, inc=1, device_id={"chan": device}, device_id_type=MESH)

    greet(across)
    greet(partner)
    pl.when(has_prev)(lambda: greet(prev))
    pl.when(has_next)(lambda: greet(following))
    slant_out, slant_in = (x == 0) & has_prev, (x == 1) & has_next
    pl.when(slant_out)(lambda: greet(i - 2))
    pl.when(slant_in)(lambda: greet(i + 2))
    late = max(0, windows - 2)

    load(windows - 1).start()
    for t in first_tables:
        fetch(t).start()
    load(windows - 2).start()
    for t in later_tables:
        fetch(t).start()
    for w in reversed(range(windows - 2)):
        load(w).start()

    def all_here():
        others = sum(flag.astype(jnp.int32) for flag in (has_prev, has_next, slant_out, slant_in))
        pl.semaphore_wait(barrier, 2 + others)

    def copy(item, k, source, slot, device):
        return pltpu.make_async_remote_copy(
            src_ref=feats.at[source, k],
            dst_ref=feats.at[slot, k],
            send_sem=send.at[item, k],
            recv_sem=recv.at[slot, k],
            device_id={"chan": device},
            device_id_type=MESH,
        )

    def arrived(slot, k):
        pltpu.make_async_copy(feats.at[slot, k], feats.at[slot, k], recv.at[slot, k]).wait()

    def left(item, k):
        pltpu.make_async_copy(feats.at[0, k], feats.at[0, k], send.at[item, k]).wait()

    def send_own(k):
        pl.when(has_prev)(lambda: copy(0, k, 0, 4, prev).start())
        pl.when(x == 1)(lambda: copy(2, k, 0, 2, across).start())
        pl.when(c == 1)(lambda: copy(4, k, 0, 1, partner).start())

    def forward_next(k, here):
        @pl.when(here & has_next)
        def _():
            arrived(4, k)
            pl.when(has_prev)(lambda: copy(1, k, 4, 8, prev).start())
            pl.when(slant_out & (k >= late))(lambda: copy(8, k, 4, 6, i - 2).start())
            copy(2 + x, k, 4, 2 + 4 * x, across).start()
            copy(4 + c, k, 4, 3 + 2 * c, partner).start()

    def relay_near(k, here):
        @pl.when(here & (i + 2 < devices))
        def _():
            arrived(2, k)
            copy(6, k, 2, 1 + 2 * c, partner).start()

    def forward_third(k, here):
        @pl.when(here & has_third)
        def _():
            arrived(8, k)
            pl.when((x == 0) & (k < late))(lambda: copy(3, k, 8, 6, across).start())
            pl.when(c == 0)(lambda: copy(5, k, 8, 7, partner).start())

    def relay_far(k, here):
        @pl.when(here & (i + 6 < devices))
        def _():
            arrived(6, k)
            copy(7, k, 6, 5 + 2 * c, partner).start()

    def there(k):
        return (k >= 0) & (k < windows)

    def mid_tick(n):
        k = n - FIRST
        forward_next(k, there(k))
        k = n - FIRST - 1
        relay_near(k, there(k) & (x == 0))
        k = n - THIRD
        relay_far(k, there(k) & (k < late) & (x == 1))

    def end_tick(n):
        k = n - SECOND
        forward_third(k, there(k))
        relay_near(k, there(k) & (x == 1))
        relay_far(k, there(k) & ((x == 0) | (k >= late)))

    for slot in range(1, 9):
        @pl.when(i + slot >= devices)
        def _(slot=slot):
            feats[slot] = jnp.zeros(feats.shape[1:], BF)

    def rotate(k):
        real, imag = feats[0, k, :, :NF].astype(F32), feats[0, k, :, NF:].astype(F32)

        def put(t, a, b):
            rot[k, t * channels:(t + 1) * channels, :NF] = a.astype(BF)
            rot[k, t * channels:(t + 1) * channels, NF:] = b.astype(BF)

        put(half, real, imag)
        for step in range(1, half + 1):
            t = half - step
            co, si = lag_ref[0, t:t + 1, :], lag_ref[1, t:t + 1, :]
            rc, rs, ic, js = real * co, real * si, imag * co, imag * si
            put(t, rc - js, rs + ic)
            if half + step < lags:
                put(half + step, rc + js, ic - rs)

    def side(ref, units):
        return jnp.concatenate([ref(k) for k in units], axis=1)

    def product(units):
        return lax.dot_general(
            side(lambda k: jnp.concatenate([feats[1:9, k].reshape(8 * channels, 2 * NF), feats[0, k]], axis=0), units),
            side(lambda k: rot[k], units), (((1,), (1,)), ((), ())), preferred_element_type=F32)

    def multiply(units):
        for k in units:
            for slot in (1, 3, 5, 7):
                pl.when(i + slot < devices)(lambda slot=slot, k=k: arrived(slot, k))
        products = product(units)
        if units[0] == 0:
            total[...] = products
        else:
            total[...] += products

    channel = lax.broadcasted_iota(jnp.int32, (channels, 1), 0)
    dead = jnp.zeros((channels, 1), jnp.int32)
    for j in range(channels):
        dead = jnp.where(channel == j, dead_ref[j], dead)
    alive = (1 - dead).astype(F32)
    fetch(1).wait()
    fetch(8).wait()
    prepare_windows(windows, off_ref, taper_ref, bin_ref, cosw, turn)
    held[:, :H] = jnp.zeros((channels, H), F32)
    held[:, samples + H:] = jnp.zeros((channels, H), F32)
    tail = samples // BLK * channels
    norm[tail:, :] = jnp.zeros((norm.shape[0] - tail, BLK), F32)
    fetch(0).wait()
    load(windows - 1).wait()
    mags[:, samples:] = jnp.abs(held[:, samples:]).astype(BF)

    def await_load(w):
        pl.when(w == 0)(lambda: load(0).wait())
        if windows > 2:
            pl.when(w > 0)(lambda: pltpu.make_async_copy(
                records.at[:, pl.ds(H, HOP)], held.at[:, pl.ds(H, HOP)], loaded.at[w]).wait())

    normalise_window(windows - 1, box_ref, held, mags, norm)
    fold_window(windows - 1, off_ref, norm, cosw, *folded[:4])
    load(windows - 2).wait()
    normalise_window(windows - 2, box_ref, held, mags, norm)

    def produce(n, now, later):
        w = windows - 1 - n
        pl.when(w > 1)(lambda: await_load(w - 2))
        mid_tick(n)
        parts = [transform(now[:2], te_hi, te_lo, tw_ref, 0)]
        fold_window(jnp.maximum(w - 1, 0), off_ref, norm, cosw, *later)
        parts.append(transform(now[2:], to_hi, to_lo, tw_ref, 1))
        normalise_window(jnp.maximum(w - 2, 0), box_ref, held, mags, norm)
        rotate(jnp.maximum(n - 1, 0))
        real, imag = whiten(w, parts, alive, band_ref, bin_ref, turn)
        feats[0, n, :, :NF] = real
        feats[0, n, :, NF:] = imag
        send_own(n)
        end_tick(n)

    for t in later_tables:
        fetch(t).wait()
    all_here()

    @pl.loop(0, windows // 2)
    def _(m):
        produce(2 * m, folded[:4], folded[4:])
        produce(2 * m + 1, folded[4:], folded[:4])

    rotate(windows - 1)
    pairs = [range(k, k + 2) for k in range(0, windows, 2)]
    early = [[k for pair in pairs[:-2] for k in pair], pairs[-2], pairs[-1][:1]]
    def hook_of(units):
        return max([2 * (k + SECOND) + 1 for k in units] + [2 * (k + THIRD) for k in units if k < late])

    tasks = []
    tasks += [(hook_of(units), lambda u=units: multiply(u)) for units in early]
    for hook in range(2 * windows, 2 * max(windows + SECOND, late + THIRD)):
        (end_tick if hook % 2 else mid_tick)(hook // 2)
        if tasks and tasks[0][0] <= hook:
            tasks.pop(0)[1]()
    for _, task in tasks:
        task()
    multiply(pairs[-1][1:])

    @pl.loop(0, windows)
    def _(k):
        pl.when(has_prev)(lambda: left(0, k))
        pl.when(has_prev & has_next)(lambda: left(1, k))
        pl.when((i + 4 - 4 * x < devices))(lambda: left(2, k))
        pl.when(jnp.where(x == 1, has_next, has_third & (k < late)))(lambda: left(3, k))
        for item, source in ((4, 4 - 4 * c), (5, 8 - 4 * c), (6, 2), (7, 6)):
            pl.when(i + source < devices)(lambda item=item: left(item, k))
        pl.when(slant_out & has_next & (k >= late))(lambda: left(8, k))


def whole(records, dead_mask, offsets, lags, devices):
    channels, samples = records.shape
    windows = samples // HOP
    count = lags.shape[1]
    consts = spectra_consts() + [lags]
    anywhere = pl.BlockSpec(memory_space=pl.ANY)
    vmem, smem = pl.BlockSpec(memory_space=pltpu.VMEM), pl.BlockSpec(memory_space=pltpu.SMEM)
    rows = NSUB * channels
    total = pl.pallas_call(
        functools.partial(whole_kernel, devices, windows),
        out_shape=pltpu.VMEM((9 * channels, count * channels), F32),
        in_specs=[anywhere, smem, smem] + [anywhere] * len(consts),
        out_specs=vmem,
        scratch_shapes=[
            pltpu.VMEM((9, windows, channels, 2 * NF), BF),
            pltpu.VMEM((windows, count * channels, 2 * NF), BF),
            pltpu.SemaphoreType.DMA((9, windows)),
            pltpu.SemaphoreType.DMA((9, windows)),
            pltpu.VMEM((channels, samples + 2 * H), F32),
            pltpu.SemaphoreType.DMA((windows,)),
            pltpu.VMEM((channels, samples + 2 * H), BF),
            pltpu.VMEM(((samples + HOP + JIT) // BLK * channels, BLK), F32),
            pltpu.VMEM((8 * windows, HALF), F32),
            pltpu.VMEM((2, 8 * windows, NF), F32),
        ] + [pltpu.VMEM((rows, SUB), BF)] * 8
        + [pltpu.VMEM(table.shape, table.dtype) for table in consts]
        + [pltpu.SemaphoreType.DMA((len(consts),))],
        compiler_params=pltpu.CompilerParams(
            collective_id=0, has_side_effects=True, vmem_limit_bytes=56 << 20),
        name="correlate",
    )(records, dead_mask, offsets, *consts)
    return pl.pallas_call(
        functools.partial(align_kernel, 1.0 / math.sqrt(2.0 * NF * windows)),
        out_shape=jax.ShapeDtypeStruct((count, channels, NPART), BF),
        in_specs=[vmem],
        out_specs=pl.BlockSpec(memory_space=pl.ANY),
        scratch_shapes=[
            pltpu.VMEM((count, channels, NPART), BF),
            pltpu.SemaphoreType.DMA((count // GROUP,)),
        ],
        compiler_params=pltpu.CompilerParams(vmem_limit_bytes=8 << 20),
        name="align",
    )(total)


def shifted(value, axis, steps):
    count = lax.axis_size(axis)
    leading, last = (max(0, -steps), min(count, count - steps))
    return lax.ppermute(value, axis, [(source, source + steps) for source in range(leading, last)])


def local(records, dead_mask, offsets):
    channels, samples = records.shape
    tm_count = lax.axis_size("tm")
    tm_index = lax.axis_index("tm")
    windows = samples // HOP
    lags = jnp.asarray(lag_table())
    devices = lax.axis_size("chan")
    if tm_count == 1:
        return whole(records, dead_mask, offsets, lags, devices)
    left = shifted(records[:, -H:], "tm", 1)
    right = shifted(records[:, :HOP + JIT + H], "tm", -1)
    values = jnp.concatenate([left, records, right], axis=1)
    own_offsets = lax.dynamic_slice_in_dim(offsets, tm_index * windows, windows, 0)
    own = spectra(values, dead_mask, own_offsets, True, samples, windows)
    own = lax.all_gather(own, "tm", axis=0, tiled=True)
    lags_local = NLAG // tm_count
    lags = lax.dynamic_slice_in_dim(lags, tm_index * lags_local, lags_local, 1)
    return correlate(own, lags, devices)


def solution(mesh):
    return jax.shard_map(
        local,
        mesh=mesh,
        in_specs=(P(("win", "chan"), "tm"), P(("win", "chan")), P("win")),
        out_specs=P("tm", ("win", "chan"), None),
        check_vma=False,
    )
```

```python
import functools
import math

import jax
import jax.numpy as jnp
import numpy as np
from jax import lax
from jax.experimental import pallas as pl
from jax.experimental.pallas import tpu as pltpu
from jax.sharding import PartitionSpec as P

L = 8192
HOP = 4096
JIT = 512
H = 128
K0 = 32
NF = 256
WB = 64
NLAG = 32
NPART = 256

EPS = 1e-05
BLK = 256
SUB = 512
HALF = L // 2
NSUB = HALF // SUB
HB = NF // 2
ROWS = 16
CW = 2
CHUNK = 2 * CW * NF
MESH = pl.DeviceIdType.MESH
FIRST, SECOND, THIRD = 4, 6, 9
BF = jnp.bfloat16
F32 = jnp.float32

BINS = np.concatenate([np.arange(0, NF, 2), np.arange(1, NF, 2)])


def split_np(value):
    high = value.astype(jnp.bfloat16)
    low = (value - high.astype(np.float64)).astype(jnp.bfloat16)
    return high, low


def transform_tables():
    tables = []
    for parity in range(2):
        k = K0 + np.arange(parity, NF, 2)
        angle = 2 * np.pi * ((np.arange(SUB)[:, None] * k[None, :]) % L) / L
        tables.extend(split_np(np.concatenate([np.cos(angle), -np.sin(angle)], axis=1)))
    return tables


def twiddle_table():
    rows = []
    for parity in range(2):
        k = K0 + np.arange(parity, NF, 2)
        for a in range(NSUB):
            angle = 2 * np.pi * ((SUB * a * k) % L) / L
            rows.append(0.5 * np.cos(angle))
            rows.append(0.5 * np.sin(angle))
    return np.stack(rows).astype(np.float32)


def box_table():
    i = np.arange(BLK + 2 * H)[:, None]
    j = np.arange(BLK)[None, :] + H
    return (np.abs(i - j) <= H).astype(jnp.bfloat16)


def taper_table():
    angle = 2 * np.pi * np.arange(HALF) / L
    return np.stack([np.cos(angle), np.sin(angle)]).astype(np.float32)


def band_table():
    return (np.abs(BINS[:, None] - BINS[None, :]) <= WB).astype(jnp.bfloat16)


def bin_table():
    q = np.arange(NF)
    counts = (np.abs(q[:, None] - q[None, :]) <= WB).sum(axis=0)[BINS]
    return np.stack([K0 + BINS, counts]).astype(np.int32)


def split(value):
    high = value.astype(BF)
    return high, (value - high.astype(F32)).astype(BF)


def mm(a, b):
    return jnp.dot(a, b, preferred_element_type=F32)


def spectra_group(padded, blocks, windows, group, prepare, store, hook, x_ref, dead_ref, off_ref, box_ref,
                  taper_ref, te_hi, te_lo, to_hi, to_lo, tw_ref, band_ref, bin_ref, norm, cosw, turn, e_hi,
                  e_lo, o_hi, o_lo, ye, yo):
    tail = norm.shape[0] - blocks * ROWS

    @pl.when(prepare)
    def _():
        window = lax.broadcasted_iota(jnp.int32, (windows, 1), 0)
        off = jnp.zeros((windows, 1), jnp.int32)
        for w in range(windows):
            off = jnp.where(window == w, off_ref[w], off)
        angle = off.astype(F32) * (2.0 * math.pi / L)
        cosw[...] = taper_ref[0:1, :] * jnp.cos(angle) + taper_ref[1:2, :] * jnp.sin(angle)
        turns = ((off * bin_ref[0:1, :]) & (L - 1)).astype(F32) * (2.0 * math.pi / L)
        turn[0] = jnp.cos(turns)
        turn[1] = jnp.sin(turns)
        if tail:
            norm[blocks * ROWS:, :] = jnp.zeros((tail, BLK), F32)

    channel = lax.broadcasted_iota(jnp.int32, (ROWS, 1), 0)
    dead = jnp.zeros((ROWS, 1), jnp.int32)
    for c in range(ROWS):
        dead = jnp.where(channel == c, dead_ref[group * ROWS + c], dead)
    alive = (1 - dead).astype(F32)
    per = 16
    shift = H if padded else 0

    def normalise(first, count, left_edge, right_edge):
        mags, vals = [], []
        for i in range(count):
            base = (first + i) * BLK + shift
            at = base if isinstance(base, int) else pl.multiple_of(base, 128)
            vals.append(x_ref[:, pl.ds(at, BLK)] * alive)
            pieces = []
            lo = base - H if isinstance(base, int) else pl.multiple_of(base - H, 128)
            if left_edge and i == 0:
                pieces = [jnp.zeros((ROWS, H), F32), x_ref[:, pl.ds(at, BLK + H)]]
            elif right_edge and i == count - 1:
                pieces = [x_ref[:, pl.ds(lo, BLK + H)], jnp.zeros((ROWS, H), F32)]
            else:
                pieces = [x_ref[:, pl.ds(lo, BLK + 2 * H)]]
            piece = pieces[0] if len(pieces) == 1 else jnp.concatenate(pieces, axis=1)
            mags.append(jnp.abs(piece * alive).astype(BF))
        level = mm(jnp.concatenate(mags, axis=0), box_ref[...]) * (1.0 / (2 * H + 1))
        value = jnp.concatenate(vals, axis=0) / (level + EPS)
        at = first * ROWS if isinstance(first, int) else pl.multiple_of(first * ROWS, ROWS)
        norm[pl.ds(at, count * ROWS), :] = value

    if padded:
        full = blocks // per

        @pl.loop(0, full)
        def _(i):
            normalise(i * per, per, False, False)

        if blocks % per:
            normalise(full * per, blocks % per, False, False)
    else:
        normalise(0, per, True, blocks == per)

        @pl.loop(1, blocks // per - 1)
        def _(i):
            normalise(i * per, per, False, False)

        if blocks > per:
            normalise(blocks - per, per, False, True)

    lane = lax.broadcasted_iota(jnp.int32, (ROWS, BLK), 1)
    hop_blocks = HOP // BLK

    @pl.loop(0, windows)
    def _(w):
        base = w * hop_blocks

        def block(i):
            return norm[pl.ds(pl.multiple_of((base + i) * ROWS, ROWS), ROWS), :]

        off_w = off_ref[w]
        for a in range(NSUB):
            for h in range(SUB // BLK):
                i = a * (SUB // BLK) + h
                first = block(i)
                if i * BLK < JIT:
                    first = jnp.where(lane + i * BLK < off_w, block(i + 2 * hop_blocks), first)
                second = block(i + hop_blocks)
                cosine = cosw[pl.ds(w, 1), i * BLK:(i + 1) * BLK]
                total, delta = first + second, first - second
                cols = slice(h * BLK, (h + 1) * BLK)
                at = pl.ds(pl.multiple_of((w * NSUB + a) * ROWS, ROWS), ROWS)
                e_hi[at, cols], e_lo[at, cols] = split(total - cosine * delta)
                o_hi[at, cols], o_lo[at, cols] = split(delta - cosine * total)

    hook(0)
    ye[...] = mm(e_hi[...], te_hi[...]) + mm(e_hi[...], te_lo[...]) + mm(e_lo[...], te_hi[...])
    hook(1)
    yo[...] = mm(o_hi[...], to_hi[...]) + mm(o_hi[...], to_lo[...]) + mm(o_lo[...], to_hi[...])

    hook(2)
    inverse = 1.0 / bin_ref[1:2, :].astype(F32)
    reals, imags = [], []
    for w in range(windows):
        parts = []
        for parity, y in ((0, ye), (1, yo)):
            real = imag = None
            for a in range(NSUB):
                at = (w * NSUB + a) * ROWS
                yr, yi = y[at:at + ROWS, :HB], y[at:at + ROWS, HB:]
                row = (parity * NSUB + a) * 2
                c, s = tw_ref[row:row + 1, :], tw_ref[row + 1:row + 2, :]
                r, m = yr * c + yi * s, yi * c - yr * s
                real, imag = (r, m) if real is None else (real + r, imag + m)
            parts.append((real, imag))
        real = jnp.concatenate([parts[0][0], parts[1][0]], axis=1)
        imag = jnp.concatenate([parts[0][1], parts[1][1]], axis=1)
        c, s = turn[0, w:w + 1, :], turn[1, w:w + 1, :]
        reals.append(real * c - imag * s)
        imags.append(real * s + imag * c)
    real, imag = jnp.concatenate(reals, axis=0), jnp.concatenate(imags, axis=0)
    mag_hi, mag_lo = split(jnp.sqrt(real * real + imag * imag + 1e-12))
    smooth = (mm(mag_hi, band_ref[...]) + mm(mag_lo, band_ref[...])) * inverse + EPS
    white = ((real / smooth).astype(BF), (imag / smooth).astype(BF))
    for part in range(2):
        for w in range(windows):
            at = (part * CW + w % CW) * NF
            store(w // CW, at, white[part][w * ROWS:(w + 1) * ROWS, :])


def spectra_kernel(padded, blocks, windows, x_ref, dead_ref, off_ref, *refs):
    out_ref = refs[9]

    def store(k, at, value):
        out_ref[k, :, at:at + NF] = value

    spectra_group(padded, blocks, windows, pl.program_id(0), pl.program_id(0) == 0, store, lambda stage: None,
                  x_ref, dead_ref, off_ref, *refs[:9], *refs[10:])


def spectra_consts():
    tables = [box_table(), taper_table(), *transform_tables(), twiddle_table(), band_table(), bin_table()]
    return [jnp.asarray(t) for t in tables]


def spectra_scratch(norm_blocks, windows):
    rows = windows * NSUB * ROWS
    return [
        pltpu.VMEM((norm_blocks * ROWS, BLK), F32),
        pltpu.VMEM((windows, HALF), F32),
        pltpu.VMEM((2, windows, NF), F32),
    ] + [pltpu.VMEM((rows, SUB), BF)] * 4 + [pltpu.VMEM((rows, NF), F32)] * 2


def spectra(samples_in, dead_mask, offsets, padded, samples, windows):
    channels, width = samples_in.shape
    blocks = (samples + (HOP + JIT if padded else 0)) // BLK
    norm_blocks = (samples + HOP + JIT) // BLK
    consts = spectra_consts()
    whole = [pl.BlockSpec(c.shape, lambda i: (0, 0)) for c in consts]
    return pl.pallas_call(
        functools.partial(spectra_kernel, padded, blocks, windows),
        grid=(channels // ROWS,),
        out_shape=jax.ShapeDtypeStruct((windows // CW, channels, CHUNK), BF),
        in_specs=[
            pl.BlockSpec((ROWS, width), lambda i: (i, 0)),
            pl.BlockSpec(memory_space=pltpu.SMEM),
            pl.BlockSpec(memory_space=pltpu.SMEM),
        ] + whole,
        out_specs=pl.BlockSpec((windows // CW, ROWS, CHUNK), lambda i: (0, i, 0)),
        scratch_shapes=spectra_scratch(norm_blocks, windows),
        compiler_params=pltpu.CompilerParams(vmem_limit_bytes=56 << 20),
        name="spectra",
    )(samples_in, dead_mask, offsets, *consts)


def lag_table():
    lags = np.arange(NLAG) - NLAG // 2
    angle = 2 * np.pi * ((lags[:, None] * (K0 + BINS)[None, :]) % L) / L
    return np.stack([np.cos(angle), np.sin(angle)]).astype(np.float32)


GROUP = 8


def correlate_kernel(scale, devices, produce, own_ref, lag_ref, out_ref, feats, rot, total, send, recv):
    _, chunks, channels, _ = feats.shape
    per = chunks // 2
    groups = channels // ROWS
    units = 2 * groups
    lags = out_ref.shape[0]
    i = lax.axis_index("chan")
    r = lax.rem(i, 4)
    x, c = r // 2, lax.rem(r, 2)
    has_prev, has_next, has_third = i >= 4, i + 4 < devices, i + 8 < devices
    prev, following = i - 4, i + 4
    across, partner = i + 2 - 4 * x, i + 1 - 2 * c

    barrier = pltpu.get_barrier_semaphore()

    def greet(device):
        pl.semaphore_signal(barrier, inc=1, device_id={"chan": device}, device_id_type=MESH)

    greet(across)
    greet(partner)
    pl.when(has_prev)(lambda: greet(prev))
    pl.when(has_next)(lambda: greet(following))

    def all_here():
        pl.semaphore_wait(barrier, 2 + has_prev.astype(jnp.int32) + has_next.astype(jnp.int32))

    def unit(slot, k):
        return feats.at[slot, pl.ds(k % 2 * per, per), pl.ds(k // 2 * ROWS, ROWS)]

    def copy(item, k, source, slot, device):
        return pltpu.make_async_remote_copy(
            src_ref=unit(source, k),
            dst_ref=unit(slot, k),
            send_sem=send.at[item, k],
            recv_sem=recv.at[slot, k],
            device_id={"chan": device},
            device_id_type=MESH,
        )

    def arrived(slot, k):
        pltpu.make_async_copy(unit(slot, k), unit(slot, k), recv.at[slot, k]).wait()

    def left(item, k):
        pltpu.make_async_copy(unit(0, k), unit(0, k), send.at[item, k]).wait()

    def send_own(k):
        pl.when(has_prev)(lambda: copy(0, k, 0, 4, prev).start())
        pl.when(x == 1)(lambda: copy(2, k, 0, 2, across).start())
        pl.when(c == 1)(lambda: copy(4, k, 0, 1, partner).start())

    def first_forward(k):
        @pl.when(has_next)
        def _():
            arrived(4, k)
            pl.when(has_prev)(lambda: copy(1, k, 4, 8, prev).start())
            copy(2 + x, k, 4, 2 + 4 * x, across).start()
            copy(4 + c, k, 4, 3 + 2 * c, partner).start()

    def first_relay(k):
        @pl.when(i + 2 < devices)
        def _():
            arrived(2, k)
            copy(6, k, 2, 1 + 2 * c, partner).start()

    def last_forward(k):
        @pl.when(has_third)
        def _():
            arrived(8, k)
            pl.when(x == 0)(lambda: copy(3, k, 8, 6, across).start())
            pl.when(c == 0)(lambda: copy(5, k, 8, 7, partner).start())

    def last_relay(k):
        @pl.when(i + 6 < devices)
        def _():
            arrived(6, k)
            copy(7, k, 6, 5 + 2 * c, partner).start()

    for slot in range(1, 9):
        @pl.when(i + slot >= devices)
        def _(slot=slot):
            feats[slot] = jnp.zeros(feats.shape[1:], BF)

    size = GROUP * channels
    row = lax.broadcasted_iota(jnp.int32, (size, size), 0)
    col = lax.broadcasted_iota(jnp.int32, (size, size), 1)
    within = lax.rem(row, channels)
    flip = (col == row - within + (channels - 1 - within)).astype(F32).astype(BF)

    def rotate(k):
        backward = mm(flip[:channels, :channels], feats[0, k])
        for w in range(CW):
            lo, hi = w * NF, (CW + w) * NF
            real, imag = backward[:, lo:lo + NF], backward[:, hi:hi + NF]

            @pl.loop(0, lags, unroll=4)
            def _(t):
                co, si = lag_ref[0, pl.ds(t, 1), :], lag_ref[1, pl.ds(t, 1), :]
                at = pl.ds(pl.multiple_of(t * channels, channels), channels)
                rot[k, at, lo:lo + NF] = (real * co - imag * si).astype(BF)
                rot[k, at, hi:hi + NF] = (real * si + imag * co).astype(BF)

    def multiply(k):
        products = lax.dot_general(
            rot[k], feats[:, k].reshape(9 * channels, CHUNK), (((1,), (1,)), ((), ())),
            preferred_element_type=F32)
        if k == 0:
            total[...] = products
        elif k < chunks - 1:
            total[...] += products
        else:
            total[...] = (total[...] + products) * scale

    def odd_arrived(k):
        for slot in (1, 3, 5, 7):
            pl.when(i + slot < devices)(lambda slot=slot: arrived(slot, k))

    if produce is None:
        all_here()
        for k in range(chunks):
            feats[0, k] = own_ref[k]
        for k in range(units):
            send_own(k)
        early = 0
    else:
        def stages(stage):
            if stage < 2:
                first_forward(stage)
            else:
                first_relay(0)
                first_relay(1)

        produce(0, lambda stage: None)
        all_here()
        send_own(0)
        send_own(1)
        for group in range(1, groups):
            produce(group, stages if group == 1 else lambda stage: None)
            send_own(2 * group)
            send_own(2 * group + 1)
        early = 2
    turns = iter(range(chunks))

    def turn_some(count):
        for _ in range(count):
            k = next(turns, None)
            if k is not None:
                rotate(k)

    for k in range(early):
        last_forward(k)
    for k in range(early):
        last_relay(k)
    share = -(-chunks // max(1, units - early))
    for k in range(early, units):
        turn_some(share)
        first_forward(k)
    turn_some(chunks)
    for k in range(early, units):
        first_relay(k)
    for k in range(early):
        odd_arrived(k)
    for k in range(early, units):
        last_forward(k)
        if k > early:
            last_relay(k - 1)
    last_relay(units - 1)
    for half in range(2):
        for group in range(groups):
            if 2 * group + half >= early:
                odd_arrived(2 * group + half)
        for k in range(half * per, (half + 1) * per):
            multiply(k)

    cols = total.shape[1]
    wide = -(-cols // 128) * 128

    @pl.loop(0, lags // GROUP)
    def _(g):
        pieces = []
        for t in range(GROUP):
            at = pl.multiple_of((g * GROUP + t) * channels, channels)
            piece = total[pl.ds(at, channels), :]
            piece = jnp.concatenate([piece, jnp.zeros((channels, wide - cols), F32)], axis=1)
            piece = pltpu.roll(piece, wide - channels, 1, stride=1, stride_axis=0)
            pieces.append(piece[:, :NPART].astype(BF))
        result = mm(flip, jnp.concatenate(pieces, axis=0)).astype(BF)
        for t in range(GROUP):
            out_ref[g * GROUP + t] = result[t * channels:(t + 1) * channels, :]

    for k in range(units):
        pl.when(has_prev)(lambda k=k: left(0, k))
        pl.when(has_prev & has_next)(lambda k=k: left(1, k))
        for item, source in ((2, 4 - 4 * x), (3, 8 - 4 * x), (4, 4 - 4 * c), (5, 8 - 4 * c), (6, 2), (7, 6)):
            pl.when(i + source < devices)(lambda item=item, k=k: left(item, k))


def correlate_call(kernel, operands, specs, count, channels, chunks, extra):
    units = 2 * (channels // ROWS)
    return pl.pallas_call(
        kernel,
        out_shape=jax.ShapeDtypeStruct((count, channels, NPART), BF),
        in_specs=specs,
        out_specs=pl.BlockSpec(memory_space=pltpu.VMEM),
        scratch_shapes=[
            pltpu.VMEM((9, chunks, channels, CHUNK), BF),
            pltpu.VMEM((chunks, count * channels, CHUNK), BF),
            pltpu.VMEM((count * channels, 9 * channels), F32),
            pltpu.SemaphoreType.DMA((8, units)),
            pltpu.SemaphoreType.DMA((9, units)),
        ] + extra,
        compiler_params=pltpu.CompilerParams(
            collective_id=0, has_side_effects=True, vmem_limit_bytes=56 << 20),
        name="correlate",
    )(*operands)


def scale_of(chunks):
    return 1.0 / math.sqrt(2.0 * NF * chunks * CW)


def correlate(own, lags, devices):
    chunks, channels, _ = own.shape
    kernel = functools.partial(correlate_kernel, scale_of(chunks), devices, None)
    specs = [pl.BlockSpec(memory_space=pltpu.VMEM)] * 2
    return correlate_call(kernel, (own, lags), specs, lags.shape[1], channels, chunks, [])


def prepare_windows(windows, off_ref, taper_ref, bin_ref, cosw, turn):
    for w in range(windows):
        angle = jnp.full((8, 1), off_ref[w], jnp.int32).astype(F32) * (2.0 * math.pi / L)
        at = slice(8 * w, 8 * w + 8)
        cosw[at, :] = taper_ref[0:1, :] * jnp.cos(angle) + taper_ref[1:2, :] * jnp.sin(angle)
        turns = ((off_ref[w] * bin_ref[0:1, :]) & (L - 1)).astype(F32) * (2.0 * math.pi / L)
        turn[0, at, :] = jnp.broadcast_to(jnp.cos(turns), (8, NF))
        turn[1, at, :] = jnp.broadcast_to(jnp.sin(turns), (8, NF))


def repeat_rows(value, rows):
    return jnp.concatenate([value] * (rows // value.shape[0]), axis=0)


def normalise_window(w, box_ref, held, mags, norm):
    channels = held.shape[0]
    hop_blocks = HOP // BLK
    base = pl.multiple_of(w * HOP, HOP)

    def cols(first, count):
        return pl.ds(pl.multiple_of(base + first, 128), count)

    mags[:, cols(0, HOP)] = jnp.abs(held[:, cols(0, HOP)]).astype(BF)
    pieces = [mags[:, cols(b * BLK, BLK + 2 * H)] for b in range(hop_blocks)]
    level = mm(jnp.concatenate(pieces, axis=0), box_ref[...]) * (1.0 / (2 * H + 1)) + EPS
    values = jnp.concatenate([held[:, cols(H + b * BLK, BLK)] for b in range(hop_blocks)], axis=0)
    rows = hop_blocks * channels
    norm[pl.ds(pl.multiple_of(w * rows, rows), rows), :] = values / level


def fold_window(w, off_ref, norm, cosw, e_hi, e_lo, o_hi, o_lo):
    channels = e_hi.shape[0] // NSUB
    hop_blocks = HOP // BLK

    def block(i):
        return norm[pl.ds(pl.multiple_of((w * hop_blocks + i) * channels, channels), channels), :]

    lane = lax.broadcasted_iota(jnp.int32, (channels, BLK), 1)
    off_w = off_ref[w]
    per_w = pl.ds(pl.multiple_of(8 * w, 8), 8)
    for a in range(NSUB):
        for h in range(SUB // BLK):
            i = a * (SUB // BLK) + h
            first = block(i)
            if i * BLK < JIT:
                first = jnp.where(lane + i * BLK < off_w, block(i + 2 * hop_blocks), first)
            second = block(i + hop_blocks)
            cosine = repeat_rows(cosw[per_w, i * BLK:(i + 1) * BLK], channels)
            total, delta = first + second, first - second
            at, span = slice(a * channels, (a + 1) * channels), slice(h * BLK, (h + 1) * BLK)
            e_hi[at, span], e_lo[at, span] = split(total - cosine * delta)
            o_hi[at, span], o_lo[at, span] = split(delta - cosine * total)


def transform(folded, t_hi, t_lo, tw_ref, parity):
    hi, lo = folded
    channels = hi.shape[0] // NSUB
    y = mm(jnp.concatenate([hi[...], hi[...], lo[...]], axis=1),
           jnp.concatenate([t_hi[...], t_lo[...], t_hi[...]], axis=0))
    real = imag = None
    for a in range(NSUB):
        at = slice(a * channels, (a + 1) * channels)
        yr, yi = y[at, :HB], y[at, HB:]
        row = (parity * NSUB + a) * 2
        c, s = tw_ref[row:row + 1, :], tw_ref[row + 1:row + 2, :]
        r, m = yr * c + yi * s, yi * c - yr * s
        real, imag = (r, m) if real is None else (real + r, imag + m)
    return real, imag


def whiten(w, parts, alive, band_ref, bin_ref, turn):
    channels = alive.shape[0]
    per_w = pl.ds(pl.multiple_of(8 * w, 8), 8)
    real = jnp.concatenate([parts[0][0], parts[1][0]], axis=1)
    imag = jnp.concatenate([parts[0][1], parts[1][1]], axis=1)
    c, s = repeat_rows(turn[0, per_w, :], channels), repeat_rows(turn[1, per_w, :], channels)
    real, imag = real * c - imag * s, real * s + imag * c
    mag_hi, mag_lo = split(jnp.sqrt(real * real + imag * imag + 1e-12))
    inverse = 1.0 / bin_ref[1:2, :].astype(F32)
    smooth = (mm(mag_hi, band_ref[...]) + mm(mag_lo, band_ref[...])) * inverse + EPS
    return (real / smooth * alive).astype(BF), (imag / smooth * alive).astype(BF)


def flip_matrix(size, channels):
    row = lax.broadcasted_iota(jnp.int32, (size, size), 0)
    col = lax.broadcasted_iota(jnp.int32, (size, size), 1)
    within = lax.rem(row, channels)
    return (col == row - within + (channels - 1 - within)).astype(F32).astype(BF)


def align_kernel(scale, total, out_ref, staged, stored):
    lags, channels, _ = out_ref.shape
    size = GROUP * channels
    flip = flip_matrix(size, channels)
    far = 8 * channels

    def store(g):
        at = pl.ds(g * GROUP, GROUP)
        return pltpu.make_async_copy(staged.at[at], out_ref.at[at], stored.at[g])

    turned = []
    for g in range(lags // GROUP):
        values = (total[:, g * size:(g + 1) * size] * scale).astype(BF)
        values = jnp.concatenate(
            [values[:far], jnp.zeros((128 - channels, size), BF), values[far:]], axis=0)
        turned.append(lax.dot_general(flip, values, (((1,), (1,)), ((), ())), preferred_element_type=F32))
    for g in range(lags // GROUP):
        pieces = []
        for t in range(GROUP):
            piece = pltpu.roll(turned[g][t * channels:(t + 1) * channels, :], 0, 1, stride=1, stride_axis=0)
            pieces.append(piece[:, :NPART].astype(BF))
        result = mm(flip, jnp.concatenate(pieces, axis=0)).astype(BF)
        for t in range(GROUP):
            staged[g * GROUP + t] = result[t * channels:(t + 1) * channels, :]
        store(g).start()
    for g in range(lags // GROUP):
        store(g).wait()


def whole_kernel(devices, windows, records, dead_ref, off_ref, *refs):
    sources, total, refs = refs[:10], refs[10], refs[11:]
    feats, rot, send, recv, held, loaded, mags, norm, cosw, turn, *folded = refs[:18]
    tables, fetched = refs[18:28], refs[28]
    box_ref, taper_ref, te_hi, te_lo, to_hi, to_lo, tw_ref, band_ref, bin_ref, lag_ref = tables
    channels, samples = records.shape
    lags = lag_ref.shape[1]
    half = lags // 2
    i = lax.axis_index("chan")
    r = lax.rem(i, 4)
    x, c = r // 2, lax.rem(r, 2)
    has_prev, has_next, has_third = i >= 4, i + 4 < devices, i + 8 < devices
    prev, following = i - 4, i + 4
    across, partner = i + 2 - 4 * x, i + 1 - 2 * c

    def load(w):
        first = max(0, w * HOP - H)
        last = (w + 1) * HOP - H if w < windows - 1 else samples
        return pltpu.make_async_copy(
            records.at[:, pl.ds(first, last - first)], held.at[:, pl.ds(first + H, last - first)], loaded.at[w])

    def fetch(t):
        return pltpu.make_async_copy(sources[t], tables[t], fetched.at[t])

    first_tables, later_tables = (1, 8, 0), (2, 3, 4, 5, 6, 7, 9)

    barrier = pltpu.get_barrier_semaphore()

    def greet(device):
        pl.semaphore_signal(barrier, inc=1, device_id={"chan": device}, device_id_type=MESH)

    greet(across)
    greet(partner)
    pl.when(has_prev)(lambda: greet(prev))
    pl.when(has_next)(lambda: greet(following))
    slant_out, slant_in = (x == 0) & has_prev, (x == 1) & has_next
    pl.when(slant_out)(lambda: greet(i - 2))
    pl.when(slant_in)(lambda: greet(i + 2))
    late = max(0, windows - 2)

    load(windows - 1).start()
    for t in first_tables:
        fetch(t).start()
    load(windows - 2).start()
    for t in later_tables:
        fetch(t).start()
    for w in reversed(range(windows - 2)):
        load(w).start()

    def all_here():
        others = sum(flag.astype(jnp.int32) for flag in (has_prev, has_next, slant_out, slant_in))
        pl.semaphore_wait(barrier, 2 + others)

    def copy(item, k, source, slot, device):
        return pltpu.make_async_remote_copy(
            src_ref=feats.at[source, k],
            dst_ref=feats.at[slot, k],
            send_sem=send.at[item, k],
            recv_sem=recv.at[slot, k],
            device_id={"chan": device},
            device_id_type=MESH,
        )

    def arrived(slot, k):
        pltpu.make_async_copy(feats.at[slot, k], feats.at[slot, k], recv.at[slot, k]).wait()

    def left(item, k):
        pltpu.make_async_copy(feats.at[0, k], feats.at[0, k], send.at[item, k]).wait()

    def send_own(k):
        pl.when(has_prev)(lambda: copy(0, k, 0, 4, prev).start())
        pl.when(x == 1)(lambda: copy(2, k, 0, 2, across).start())
        pl.when(c == 1)(lambda: copy(4, k, 0, 1, partner).start())

    def forward_next(k, here):
        @pl.when(here & has_next)
        def _():
            arrived(4, k)
            pl.when(has_prev)(lambda: copy(1, k, 4, 8, prev).start())
            pl.when(slant_out & (k >= late))(lambda: copy(8, k, 4, 6, i - 2).start())
            copy(2 + x, k, 4, 2 + 4 * x, across).start()
            copy(4 + c, k, 4, 3 + 2 * c, partner).start()

    def relay_near(k, here):
        @pl.when(here & (i + 2 < devices))
        def _():
            arrived(2, k)
            copy(6, k, 2, 1 + 2 * c, partner).start()

    def forward_third(k, here):
        @pl.when(here & has_third)
        def _():
            arrived(8, k)
            pl.when((x == 0) & (k < late))(lambda: copy(3, k, 8, 6, across).start())
            pl.when(c == 0)(lambda: copy(5, k, 8, 7, partner).start())

    def relay_far(k, here):
        @pl.when(here & (i + 6 < devices))
        def _():
            arrived(6, k)
            copy(7, k, 6, 5 + 2 * c, partner).start()

    def there(k):
        return (k >= 0) & (k < windows)

    def mid_tick(n):
        k = n - FIRST
        forward_next(k, there(k))
        k = n - FIRST - 1
        relay_near(k, there(k) & (x == 0))
        k = n - THIRD
        relay_far(k, there(k) & (k < late) & (x == 1))

    def end_tick(n):
        k = n - SECOND
        forward_third(k, there(k))
        relay_near(k, there(k) & (x == 1))
        relay_far(k, there(k) & ((x == 0) | (k >= late)))

    for slot in range(1, 9):
        @pl.when(i + slot >= devices)
        def _(slot=slot):
            feats[slot] = jnp.zeros(feats.shape[1:], BF)

    def rotate(k):
        real, imag = feats[0, k, :, :NF].astype(F32), feats[0, k, :, NF:].astype(F32)

        def put(t, a, b):
            rot[k, t * channels:(t + 1) * channels, :NF] = a.astype(BF)
            rot[k, t * channels:(t + 1) * channels, NF:] = b.astype(BF)

        put(half, real, imag)
        for step in range(1, half + 1):
            t = half - step
            co, si = lag_ref[0, t:t + 1, :], lag_ref[1, t:t + 1, :]
            rc, rs, ic, js = real * co, real * si, imag * co, imag * si
            put(t, rc - js, rs + ic)
            if half + step < lags:
                put(half + step, rc + js, ic - rs)

    def side(ref, units):
        return jnp.concatenate([ref(k) for k in units], axis=1)

    def product(units):
        return lax.dot_general(
            side(lambda k: jnp.concatenate([feats[1:9, k].reshape(8 * channels, 2 * NF), feats[0, k]], axis=0), units),
            side(lambda k: rot[k], units), (((1,), (1,)), ((), ())), preferred_element_type=F32)

    def multiply(units):
        for k in units:
            for slot in (1, 3, 5, 7):
                pl.when(i + slot < devices)(lambda slot=slot, k=k: arrived(slot, k))
        products = product(units)
        if units[0] == 0:
            total[...] = products
        else:
            total[...] += products

    channel = lax.broadcasted_iota(jnp.int32, (channels, 1), 0)
    dead = jnp.zeros((channels, 1), jnp.int32)
    for j in range(channels):
        dead = jnp.where(channel == j, dead_ref[j], dead)
    alive = (1 - dead).astype(F32)
    fetch(1).wait()
    fetch(8).wait()
    prepare_windows(windows, off_ref, taper_ref, bin_ref, cosw, turn)
    held[:, :H] = jnp.zeros((channels, H), F32)
    held[:, samples + H:] = jnp.zeros((channels, H), F32)
    tail = samples // BLK * channels
    norm[tail:, :] = jnp.zeros((norm.shape[0] - tail, BLK), F32)
    fetch(0).wait()
    load(windows - 1).wait()
    mags[:, samples:] = jnp.abs(held[:, samples:]).astype(BF)

    def await_load(w):
        pl.when(w == 0)(lambda: load(0).wait())
        if windows > 2:
            pl.when(w > 0)(lambda: pltpu.make_async_copy(
                records.at[:, pl.ds(H, HOP)], held.at[:, pl.ds(H, HOP)], loaded.at[w]).wait())

    normalise_window(windows - 1, box_ref, held, mags, norm)
    fold_window(windows - 1, off_ref, norm, cosw, *folded[:4])
    load(windows - 2).wait()
    normalise_window(windows - 2, box_ref, held, mags, norm)

    def produce(n, now, later):
        w = windows - 1 - n
        pl.when(w > 1)(lambda: await_load(w - 2))
        mid_tick(n)
        parts = [transform(now[:2], te_hi, te_lo, tw_ref, 0)]
        fold_window(jnp.maximum(w - 1, 0), off_ref, norm, cosw, *later)
        parts.append(transform(now[2:], to_hi, to_lo, tw_ref, 1))
        normalise_window(jnp.maximum(w - 2, 0), box_ref, held, mags, norm)
        rotate(jnp.maximum(n - 1, 0))
        real, imag = whiten(w, parts, alive, band_ref, bin_ref, turn)
        feats[0, n, :, :NF] = real
        feats[0, n, :, NF:] = imag
        send_own(n)
        end_tick(n)

    for t in later_tables:
        fetch(t).wait()
    all_here()

    @pl.loop(0, windows // 2)
    def _(m):
        produce(2 * m, folded[:4], folded[4:])
        produce(2 * m + 1, folded[4:], folded[:4])

    rotate(windows - 1)
    pairs = [range(k, k + 2) for k in range(0, windows, 2)]
    early = [[k for pair in pairs[:-2] for k in pair], range(windows - 4, windows - 1)]
    def hook_of(units):
        return max([2 * (k + SECOND) + 1 for k in units] + [2 * (k + THIRD) for k in units if k < late])

    tasks = []
    tasks += [(hook_of(units), lambda u=units: multiply(u)) for units in early]
    for hook in range(2 * windows, 2 * max(windows + SECOND, late + THIRD)):
        (end_tick if hook % 2 else mid_tick)(hook // 2)
        if tasks and tasks[0][0] <= hook:
            tasks.pop(0)[1]()
    for _, task in tasks:
        task()
    @pl.loop(0, windows)
    def _(k):
        pl.when(has_prev)(lambda: left(0, k))
        pl.when(has_prev & has_next)(lambda: left(1, k))
        pl.when((i + 4 - 4 * x < devices))(lambda: left(2, k))
        pl.when(jnp.where(x == 1, has_next, has_third & (k < late)))(lambda: left(3, k))
        for item, source in ((4, 4 - 4 * c), (5, 8 - 4 * c), (6, 2), (7, 6)):
            pl.when(i + source < devices)(lambda item=item: left(item, k))
        pl.when(slant_out & has_next & (k >= late))(lambda: left(8, k))

    multiply(pairs[-1][1:])


def whole(records, dead_mask, offsets, lags, devices):
    channels, samples = records.shape
    windows = samples // HOP
    count = lags.shape[1]
    consts = spectra_consts() + [lags]
    anywhere = pl.BlockSpec(memory_space=pl.ANY)
    vmem, smem = pl.BlockSpec(memory_space=pltpu.VMEM), pl.BlockSpec(memory_space=pltpu.SMEM)
    rows = NSUB * channels
    total = pl.pallas_call(
        functools.partial(whole_kernel, devices, windows),
        out_shape=pltpu.VMEM((9 * channels, count * channels), F32),
        in_specs=[anywhere, smem, smem] + [anywhere] * len(consts),
        out_specs=vmem,
        scratch_shapes=[
            pltpu.VMEM((9, windows, channels, 2 * NF), BF),
            pltpu.VMEM((windows, count * channels, 2 * NF), BF),
            pltpu.SemaphoreType.DMA((9, windows)),
            pltpu.SemaphoreType.DMA((9, windows)),
            pltpu.VMEM((channels, samples + 2 * H), F32),
            pltpu.SemaphoreType.DMA((windows,)),
            pltpu.VMEM((channels, samples + 2 * H), BF),
            pltpu.VMEM(((samples + HOP + JIT) // BLK * channels, BLK), F32),
            pltpu.VMEM((8 * windows, HALF), F32),
            pltpu.VMEM((2, 8 * windows, NF), F32),
        ] + [pltpu.VMEM((rows, SUB), BF)] * 8
        + [pltpu.VMEM(table.shape, table.dtype) for table in consts]
        + [pltpu.SemaphoreType.DMA((len(consts),))],
        compiler_params=pltpu.CompilerParams(
            collective_id=0, has_side_effects=True, vmem_limit_bytes=56 << 20),
        name="correlate",
    )(records, dead_mask, offsets, *consts)
    return pl.pallas_call(
        functools.partial(align_kernel, 1.0 / math.sqrt(2.0 * NF * windows)),
        out_shape=jax.ShapeDtypeStruct((count, channels, NPART), BF),
        in_specs=[vmem],
        out_specs=pl.BlockSpec(memory_space=pl.ANY),
        scratch_shapes=[
            pltpu.VMEM((count, channels, NPART), BF),
            pltpu.SemaphoreType.DMA((count // GROUP,)),
        ],
        compiler_params=pltpu.CompilerParams(vmem_limit_bytes=8 << 20),
        name="align",
    )(total)


def shifted(value, axis, steps):
    count = lax.axis_size(axis)
    leading, last = (max(0, -steps), min(count, count - steps))
    return lax.ppermute(value, axis, [(source, source + steps) for source in range(leading, last)])


def local(records, dead_mask, offsets):
    channels, samples = records.shape
    tm_count = lax.axis_size("tm")
    tm_index = lax.axis_index("tm")
    windows = samples // HOP
    lags = jnp.asarray(lag_table())
    devices = lax.axis_size("chan")
    if tm_count == 1:
        return whole(records, dead_mask, offsets, lags, devices)
    left = shifted(records[:, -H:], "tm", 1)
    right = shifted(records[:, :HOP + JIT + H], "tm", -1)
    values = jnp.concatenate([left, records, right], axis=1)
    own_offsets = lax.dynamic_slice_in_dim(offsets, tm_index * windows, windows, 0)
    own = spectra(values, dead_mask, own_offsets, True, samples, windows)
    own = lax.all_gather(own, "tm", axis=0, tiled=True)
    lags_local = NLAG // tm_count
    lags = lax.dynamic_slice_in_dim(lags, tm_index * lags_local, lags_local, 1)
    return correlate(own, lags, devices)


def solution(mesh):
    return jax.shard_map(
        local,
        mesh=mesh,
        in_specs=(P(("win", "chan"), "tm"), P(("win", "chan")), P("win")),
        out_specs=P("tm", ("win", "chan"), None),
        check_vma=False,
    )
```

```python
import functools
import math

import jax
import jax.numpy as jnp
import numpy as np
from jax import lax
from jax.experimental import pallas as pl
from jax.experimental.pallas import tpu as pltpu
from jax.sharding import PartitionSpec as P

L = 8192
HOP = 4096
JIT = 512
H = 128
K0 = 32
NF = 256
WB = 64
NLAG = 32
NPART = 256

EPS = 1e-05
BLK = 256
SUB = 512
HALF = L // 2
NSUB = HALF // SUB
HB = NF // 2
ROWS = 16
CW = 2
CHUNK = 2 * CW * NF
MESH = pl.DeviceIdType.MESH
FIRST, SECOND, THIRD = 4, 6, 9
BF = jnp.bfloat16
F32 = jnp.float32

BINS = np.concatenate([np.arange(0, NF, 2), np.arange(1, NF, 2)])


def split_np(value):
    high = value.astype(jnp.bfloat16)
    low = (value - high.astype(np.float64)).astype(jnp.bfloat16)
    return high, low


def transform_tables():
    tables = []
    for parity in range(2):
        k = K0 + np.arange(parity, NF, 2)
        angle = 2 * np.pi * ((np.arange(SUB)[:, None] * k[None, :]) % L) / L
        tables.extend(split_np(np.concatenate([np.cos(angle), -np.sin(angle)], axis=1)))
    return tables


def twiddle_table():
    rows = []
    for parity in range(2):
        k = K0 + np.arange(parity, NF, 2)
        for a in range(NSUB):
            angle = 2 * np.pi * ((SUB * a * k) % L) / L
            rows.append(0.5 * np.cos(angle))
            rows.append(0.5 * np.sin(angle))
    return np.stack(rows).astype(np.float32)


def box_table():
    i = np.arange(BLK + 2 * H)[:, None]
    j = np.arange(BLK)[None, :] + H
    return (np.abs(i - j) <= H).astype(jnp.bfloat16)


def taper_table():
    angle = 2 * np.pi * np.arange(HALF) / L
    return np.stack([np.cos(angle), np.sin(angle)]).astype(np.float32)


def band_table():
    return (np.abs(BINS[:, None] - BINS[None, :]) <= WB).astype(jnp.bfloat16)


def bin_table():
    q = np.arange(NF)
    counts = (np.abs(q[:, None] - q[None, :]) <= WB).sum(axis=0)[BINS]
    return np.stack([K0 + BINS, counts]).astype(np.int32)


def split(value):
    high = value.astype(BF)
    return high, (value - high.astype(F32)).astype(BF)


def mm(a, b):
    return jnp.dot(a, b, preferred_element_type=F32)


def spectra_group(padded, blocks, windows, group, prepare, store, hook, x_ref, dead_ref, off_ref, box_ref,
                  taper_ref, te_hi, te_lo, to_hi, to_lo, tw_ref, band_ref, bin_ref, norm, cosw, turn, e_hi,
                  e_lo, o_hi, o_lo, ye, yo):
    tail = norm.shape[0] - blocks * ROWS

    @pl.when(prepare)
    def _():
        window = lax.broadcasted_iota(jnp.int32, (windows, 1), 0)
        off = jnp.zeros((windows, 1), jnp.int32)
        for w in range(windows):
            off = jnp.where(window == w, off_ref[w], off)
        angle = off.astype(F32) * (2.0 * math.pi / L)
        cosw[...] = taper_ref[0:1, :] * jnp.cos(angle) + taper_ref[1:2, :] * jnp.sin(angle)
        turns = ((off * bin_ref[0:1, :]) & (L - 1)).astype(F32) * (2.0 * math.pi / L)
        turn[0] = jnp.cos(turns)
        turn[1] = jnp.sin(turns)
        if tail:
            norm[blocks * ROWS:, :] = jnp.zeros((tail, BLK), F32)

    channel = lax.broadcasted_iota(jnp.int32, (ROWS, 1), 0)
    dead = jnp.zeros((ROWS, 1), jnp.int32)
    for c in range(ROWS):
        dead = jnp.where(channel == c, dead_ref[group * ROWS + c], dead)
    alive = (1 - dead).astype(F32)
    per = 16
    shift = H if padded else 0

    def normalise(first, count, left_edge, right_edge):
        mags, vals = [], []
        for i in range(count):
            base = (first + i) * BLK + shift
            at = base if isinstance(base, int) else pl.multiple_of(base, 128)
            vals.append(x_ref[:, pl.ds(at, BLK)] * alive)
            pieces = []
            lo = base - H if isinstance(base, int) else pl.multiple_of(base - H, 128)
            if left_edge and i == 0:
                pieces = [jnp.zeros((ROWS, H), F32), x_ref[:, pl.ds(at, BLK + H)]]
            elif right_edge and i == count - 1:
                pieces = [x_ref[:, pl.ds(lo, BLK + H)], jnp.zeros((ROWS, H), F32)]
            else:
                pieces = [x_ref[:, pl.ds(lo, BLK + 2 * H)]]
            piece = pieces[0] if len(pieces) == 1 else jnp.concatenate(pieces, axis=1)
            mags.append(jnp.abs(piece * alive).astype(BF))
        level = mm(jnp.concatenate(mags, axis=0), box_ref[...]) * (1.0 / (2 * H + 1))
        value = jnp.concatenate(vals, axis=0) / (level + EPS)
        at = first * ROWS if isinstance(first, int) else pl.multiple_of(first * ROWS, ROWS)
        norm[pl.ds(at, count * ROWS), :] = value

    if padded:
        full = blocks // per

        @pl.loop(0, full)
        def _(i):
            normalise(i * per, per, False, False)

        if blocks % per:
            normalise(full * per, blocks % per, False, False)
    else:
        normalise(0, per, True, blocks == per)

        @pl.loop(1, blocks // per - 1)
        def _(i):
            normalise(i * per, per, False, False)

        if blocks > per:
            normalise(blocks - per, per, False, True)

    lane = lax.broadcasted_iota(jnp.int32, (ROWS, BLK), 1)
    hop_blocks = HOP // BLK

    @pl.loop(0, windows)
    def _(w):
        base = w * hop_blocks

        def block(i):
            return norm[pl.ds(pl.multiple_of((base + i) * ROWS, ROWS), ROWS), :]

        off_w = off_ref[w]
        for a in range(NSUB):
            for h in range(SUB // BLK):
                i = a * (SUB // BLK) + h
                first = block(i)
                if i * BLK < JIT:
                    first = jnp.where(lane + i * BLK < off_w, block(i + 2 * hop_blocks), first)
                second = block(i + hop_blocks)
                cosine = cosw[pl.ds(w, 1), i * BLK:(i + 1) * BLK]
                total, delta = first + second, first - second
                cols = slice(h * BLK, (h + 1) * BLK)
                at = pl.ds(pl.multiple_of((w * NSUB + a) * ROWS, ROWS), ROWS)
                e_hi[at, cols], e_lo[at, cols] = split(total - cosine * delta)
                o_hi[at, cols], o_lo[at, cols] = split(delta - cosine * total)

    hook(0)
    ye[...] = mm(e_hi[...], te_hi[...]) + mm(e_hi[...], te_lo[...]) + mm(e_lo[...], te_hi[...])
    hook(1)
    yo[...] = mm(o_hi[...], to_hi[...]) + mm(o_hi[...], to_lo[...]) + mm(o_lo[...], to_hi[...])

    hook(2)
    inverse = 1.0 / bin_ref[1:2, :].astype(F32)
    reals, imags = [], []
    for w in range(windows):
        parts = []
        for parity, y in ((0, ye), (1, yo)):
            real = imag = None
            for a in range(NSUB):
                at = (w * NSUB + a) * ROWS
                yr, yi = y[at:at + ROWS, :HB], y[at:at + ROWS, HB:]
                row = (parity * NSUB + a) * 2
                c, s = tw_ref[row:row + 1, :], tw_ref[row + 1:row + 2, :]
                r, m = yr * c + yi * s, yi * c - yr * s
                real, imag = (r, m) if real is None else (real + r, imag + m)
            parts.append((real, imag))
        real = jnp.concatenate([parts[0][0], parts[1][0]], axis=1)
        imag = jnp.concatenate([parts[0][1], parts[1][1]], axis=1)
        c, s = turn[0, w:w + 1, :], turn[1, w:w + 1, :]
        reals.append(real * c - imag * s)
        imags.append(real * s + imag * c)
    real, imag = jnp.concatenate(reals, axis=0), jnp.concatenate(imags, axis=0)
    mag_hi, mag_lo = split(jnp.sqrt(real * real + imag * imag + 1e-12))
    smooth = (mm(mag_hi, band_ref[...]) + mm(mag_lo, band_ref[...])) * inverse + EPS
    white = ((real / smooth).astype(BF), (imag / smooth).astype(BF))
    for part in range(2):
        for w in range(windows):
            at = (part * CW + w % CW) * NF
            store(w // CW, at, white[part][w * ROWS:(w + 1) * ROWS, :])


def spectra_kernel(padded, blocks, windows, x_ref, dead_ref, off_ref, *refs):
    out_ref = refs[9]

    def store(k, at, value):
        out_ref[k, :, at:at + NF] = value

    spectra_group(padded, blocks, windows, pl.program_id(0), pl.program_id(0) == 0, store, lambda stage: None,
                  x_ref, dead_ref, off_ref, *refs[:9], *refs[10:])


def spectra_consts():
    tables = [box_table(), taper_table(), *transform_tables(), twiddle_table(), band_table(), bin_table()]
    return [jnp.asarray(t) for t in tables]


def spectra_scratch(norm_blocks, windows):
    rows = windows * NSUB * ROWS
    return [
        pltpu.VMEM((norm_blocks * ROWS, BLK), F32),
        pltpu.VMEM((windows, HALF), F32),
        pltpu.VMEM((2, windows, NF), F32),
    ] + [pltpu.VMEM((rows, SUB), BF)] * 4 + [pltpu.VMEM((rows, NF), F32)] * 2


def spectra(samples_in, dead_mask, offsets, padded, samples, windows):
    channels, width = samples_in.shape
    blocks = (samples + (HOP + JIT if padded else 0)) // BLK
    norm_blocks = (samples + HOP + JIT) // BLK
    consts = spectra_consts()
    whole = [pl.BlockSpec(c.shape, lambda i: (0, 0)) for c in consts]
    return pl.pallas_call(
        functools.partial(spectra_kernel, padded, blocks, windows),
        grid=(channels // ROWS,),
        out_shape=jax.ShapeDtypeStruct((windows // CW, channels, CHUNK), BF),
        in_specs=[
            pl.BlockSpec((ROWS, width), lambda i: (i, 0)),
            pl.BlockSpec(memory_space=pltpu.SMEM),
            pl.BlockSpec(memory_space=pltpu.SMEM),
        ] + whole,
        out_specs=pl.BlockSpec((windows // CW, ROWS, CHUNK), lambda i: (0, i, 0)),
        scratch_shapes=spectra_scratch(norm_blocks, windows),
        compiler_params=pltpu.CompilerParams(vmem_limit_bytes=56 << 20),
        name="spectra",
    )(samples_in, dead_mask, offsets, *consts)


def lag_table():
    lags = np.arange(NLAG) - NLAG // 2
    angle = 2 * np.pi * ((lags[:, None] * (K0 + BINS)[None, :]) % L) / L
    return np.stack([np.cos(angle), np.sin(angle)]).astype(np.float32)


GROUP = 8


def correlate_kernel(scale, devices, produce, own_ref, lag_ref, out_ref, feats, rot, total, send, recv):
    _, chunks, channels, _ = feats.shape
    per = chunks // 2
    groups = channels // ROWS
    units = 2 * groups
    lags = out_ref.shape[0]
    i = lax.axis_index("chan")
    r = lax.rem(i, 4)
    x, c = r // 2, lax.rem(r, 2)
    has_prev, has_next, has_third = i >= 4, i + 4 < devices, i + 8 < devices
    prev, following = i - 4, i + 4
    across, partner = i + 2 - 4 * x, i + 1 - 2 * c

    barrier = pltpu.get_barrier_semaphore()

    def greet(device):
        pl.semaphore_signal(barrier, inc=1, device_id={"chan": device}, device_id_type=MESH)

    greet(across)
    greet(partner)
    pl.when(has_prev)(lambda: greet(prev))
    pl.when(has_next)(lambda: greet(following))

    def all_here():
        pl.semaphore_wait(barrier, 2 + has_prev.astype(jnp.int32) + has_next.astype(jnp.int32))

    def unit(slot, k):
        return feats.at[slot, pl.ds(k % 2 * per, per), pl.ds(k // 2 * ROWS, ROWS)]

    def copy(item, k, source, slot, device):
        return pltpu.make_async_remote_copy(
            src_ref=unit(source, k),
            dst_ref=unit(slot, k),
            send_sem=send.at[item, k],
            recv_sem=recv.at[slot, k],
            device_id={"chan": device},
            device_id_type=MESH,
        )

    def arrived(slot, k):
        pltpu.make_async_copy(unit(slot, k), unit(slot, k), recv.at[slot, k]).wait()

    def left(item, k):
        pltpu.make_async_copy(unit(0, k), unit(0, k), send.at[item, k]).wait()

    def send_own(k):
        pl.when(has_prev)(lambda: copy(0, k, 0, 4, prev).start())
        pl.when(x == 1)(lambda: copy(2, k, 0, 2, across).start())
        pl.when(c == 1)(lambda: copy(4, k, 0, 1, partner).start())

    def first_forward(k):
        @pl.when(has_next)
        def _():
            arrived(4, k)
            pl.when(has_prev)(lambda: copy(1, k, 4, 8, prev).start())
            copy(2 + x, k, 4, 2 + 4 * x, across).start()
            copy(4 + c, k, 4, 3 + 2 * c, partner).start()

    def first_relay(k):
        @pl.when(i + 2 < devices)
        def _():
            arrived(2, k)
            copy(6, k, 2, 1 + 2 * c, partner).start()

    def last_forward(k):
        @pl.when(has_third)
        def _():
            arrived(8, k)
            pl.when(x == 0)(lambda: copy(3, k, 8, 6, across).start())
            pl.when(c == 0)(lambda: copy(5, k, 8, 7, partner).start())

    def last_relay(k):
        @pl.when(i + 6 < devices)
        def _():
            arrived(6, k)
            copy(7, k, 6, 5 + 2 * c, partner).start()

    for slot in range(1, 9):
        @pl.when(i + slot >= devices)
        def _(slot=slot):
            feats[slot] = jnp.zeros(feats.shape[1:], BF)

    size = GROUP * channels
    row = lax.broadcasted_iota(jnp.int32, (size, size), 0)
    col = lax.broadcasted_iota(jnp.int32, (size, size), 1)
    within = lax.rem(row, channels)
    flip = (col == row - within + (channels - 1 - within)).astype(F32).astype(BF)

    def rotate(k):
        backward = mm(flip[:channels, :channels], feats[0, k])
        for w in range(CW):
            lo, hi = w * NF, (CW + w) * NF
            real, imag = backward[:, lo:lo + NF], backward[:, hi:hi + NF]

            @pl.loop(0, lags, unroll=4)
            def _(t):
                co, si = lag_ref[0, pl.ds(t, 1), :], lag_ref[1, pl.ds(t, 1), :]
                at = pl.ds(pl.multiple_of(t * channels, channels), channels)
                rot[k, at, lo:lo + NF] = (real * co - imag * si).astype(BF)
                rot[k, at, hi:hi + NF] = (real * si + imag * co).astype(BF)

    def multiply(k):
        products = lax.dot_general(
            rot[k], feats[:, k].reshape(9 * channels, CHUNK), (((1,), (1,)), ((), ())),
            preferred_element_type=F32)
        if k == 0:
            total[...] = products
        elif k < chunks - 1:
            total[...] += products
        else:
            total[...] = (total[...] + products) * scale

    def odd_arrived(k):
        for slot in (1, 3, 5, 7):
            pl.when(i + slot < devices)(lambda slot=slot: arrived(slot, k))

    if produce is None:
        all_here()
        for k in range(chunks):
            feats[0, k] = own_ref[k]
        for k in range(units):
            send_own(k)
        early = 0
    else:
        def stages(stage):
            if stage < 2:
                first_forward(stage)
            else:
                first_relay(0)
                first_relay(1)

        produce(0, lambda stage: None)
        all_here()
        send_own(0)
        send_own(1)
        for group in range(1, groups):
            produce(group, stages if group == 1 else lambda stage: None)
            send_own(2 * group)
            send_own(2 * group + 1)
        early = 2
    turns = iter(range(chunks))

    def turn_some(count):
        for _ in range(count):
            k = next(turns, None)
            if k is not None:
                rotate(k)

    for k in range(early):
        last_forward(k)
    for k in range(early):
        last_relay(k)
    share = -(-chunks // max(1, units - early))
    for k in range(early, units):
        turn_some(share)
        first_forward(k)
    turn_some(chunks)
    for k in range(early, units):
        first_relay(k)
    for k in range(early):
        odd_arrived(k)
    for k in range(early, units):
        last_forward(k)
        if k > early:
            last_relay(k - 1)
    last_relay(units - 1)
    for half in range(2):
        for group in range(groups):
            if 2 * group + half >= early:
                odd_arrived(2 * group + half)
        for k in range(half * per, (half + 1) * per):
            multiply(k)

    cols = total.shape[1]
    wide = -(-cols // 128) * 128

    @pl.loop(0, lags // GROUP)
    def _(g):
        pieces = []
        for t in range(GROUP):
            at = pl.multiple_of((g * GROUP + t) * channels, channels)
            piece = total[pl.ds(at, channels), :]
            piece = jnp.concatenate([piece, jnp.zeros((channels, wide - cols), F32)], axis=1)
            piece = pltpu.roll(piece, wide - channels, 1, stride=1, stride_axis=0)
            pieces.append(piece[:, :NPART].astype(BF))
        result = mm(flip, jnp.concatenate(pieces, axis=0)).astype(BF)
        for t in range(GROUP):
            out_ref[g * GROUP + t] = result[t * channels:(t + 1) * channels, :]

    for k in range(units):
        pl.when(has_prev)(lambda k=k: left(0, k))
        pl.when(has_prev & has_next)(lambda k=k: left(1, k))
        for item, source in ((2, 4 - 4 * x), (3, 8 - 4 * x), (4, 4 - 4 * c), (5, 8 - 4 * c), (6, 2), (7, 6)):
            pl.when(i + source < devices)(lambda item=item, k=k: left(item, k))


def correlate_call(kernel, operands, specs, count, channels, chunks, extra):
    units = 2 * (channels // ROWS)
    return pl.pallas_call(
        kernel,
        out_shape=jax.ShapeDtypeStruct((count, channels, NPART), BF),
        in_specs=specs,
        out_specs=pl.BlockSpec(memory_space=pltpu.VMEM),
        scratch_shapes=[
            pltpu.VMEM((9, chunks, channels, CHUNK), BF),
            pltpu.VMEM((chunks, count * channels, CHUNK), BF),
            pltpu.VMEM((count * channels, 9 * channels), F32),
            pltpu.SemaphoreType.DMA((8, units)),
            pltpu.SemaphoreType.DMA((9, units)),
        ] + extra,
        compiler_params=pltpu.CompilerParams(
            collective_id=0, has_side_effects=True, vmem_limit_bytes=56 << 20),
        name="correlate",
    )(*operands)


def scale_of(chunks):
    return 1.0 / math.sqrt(2.0 * NF * chunks * CW)


def correlate(own, lags, devices):
    chunks, channels, _ = own.shape
    kernel = functools.partial(correlate_kernel, scale_of(chunks), devices, None)
    specs = [pl.BlockSpec(memory_space=pltpu.VMEM)] * 2
    return correlate_call(kernel, (own, lags), specs, lags.shape[1], channels, chunks, [])


def prepare_windows(windows, off_ref, taper_ref, bin_ref, cosw, turn):
    for w in range(windows):
        angle = jnp.full((8, 1), off_ref[w], jnp.int32).astype(F32) * (2.0 * math.pi / L)
        at = slice(8 * w, 8 * w + 8)
        cosw[at, :] = taper_ref[0:1, :] * jnp.cos(angle) + taper_ref[1:2, :] * jnp.sin(angle)
        turns = ((off_ref[w] * bin_ref[0:1, :]) & (L - 1)).astype(F32) * (2.0 * math.pi / L)
        turn[0, at, :] = jnp.broadcast_to(jnp.cos(turns), (8, NF))
        turn[1, at, :] = jnp.broadcast_to(jnp.sin(turns), (8, NF))


def repeat_rows(value, rows):
    return jnp.concatenate([value] * (rows // value.shape[0]), axis=0)


def normalise_window(w, box_ref, held, mags, norm):
    channels = held.shape[0]
    hop_blocks = HOP // BLK
    base = pl.multiple_of(w * HOP, HOP)

    def cols(first, count):
        return pl.ds(pl.multiple_of(base + first, 128), count)

    mags[:, cols(0, HOP)] = jnp.abs(held[:, cols(0, HOP)]).astype(BF)
    pieces = [mags[:, cols(b * BLK, BLK + 2 * H)] for b in range(hop_blocks)]
    level = mm(jnp.concatenate(pieces, axis=0), box_ref[...]) * (1.0 / (2 * H + 1)) + EPS
    values = jnp.concatenate([held[:, cols(H + b * BLK, BLK)] for b in range(hop_blocks)], axis=0)
    rows = hop_blocks * channels
    norm[pl.ds(pl.multiple_of(w * rows, rows), rows), :] = values / level


def fold_window(w, off_ref, norm, cosw, e_hi, e_lo, o_hi, o_lo):
    channels = e_hi.shape[0] // NSUB
    hop_blocks = HOP // BLK

    def block(i):
        return norm[pl.ds(pl.multiple_of((w * hop_blocks + i) * channels, channels), channels), :]

    lane = lax.broadcasted_iota(jnp.int32, (channels, BLK), 1)
    off_w = off_ref[w]
    per_w = pl.ds(pl.multiple_of(8 * w, 8), 8)
    for a in range(NSUB):
        for h in range(SUB // BLK):
            i = a * (SUB // BLK) + h
            first = block(i)
            if i * BLK < JIT:
                first = jnp.where(lane + i * BLK < off_w, block(i + 2 * hop_blocks), first)
            second = block(i + hop_blocks)
            cosine = repeat_rows(cosw[per_w, i * BLK:(i + 1) * BLK], channels)
            total, delta = first + second, first - second
            at, span = slice(a * channels, (a + 1) * channels), slice(h * BLK, (h + 1) * BLK)
            e_hi[at, span], e_lo[at, span] = split(total - cosine * delta)
            o_hi[at, span], o_lo[at, span] = split(delta - cosine * total)


def transform(folded, t_hi, t_lo, tw_ref, parity):
    hi, lo = folded
    channels = hi.shape[0] // NSUB
    y = mm(jnp.concatenate([hi[...], hi[...], lo[...]], axis=1),
           jnp.concatenate([t_hi[...], t_lo[...], t_hi[...]], axis=0))
    real = imag = None
    for a in range(NSUB):
        at = slice(a * channels, (a + 1) * channels)
        yr, yi = y[at, :HB], y[at, HB:]
        row = (parity * NSUB + a) * 2
        c, s = tw_ref[row:row + 1, :], tw_ref[row + 1:row + 2, :]
        r, m = yr * c + yi * s, yi * c - yr * s
        real, imag = (r, m) if real is None else (real + r, imag + m)
    return real, imag


def whiten(w, parts, alive, band_ref, bin_ref, turn):
    channels = alive.shape[0]
    per_w = pl.ds(pl.multiple_of(8 * w, 8), 8)
    real = jnp.concatenate([parts[0][0], parts[1][0]], axis=1)
    imag = jnp.concatenate([parts[0][1], parts[1][1]], axis=1)
    c, s = repeat_rows(turn[0, per_w, :], channels), repeat_rows(turn[1, per_w, :], channels)
    real, imag = real * c - imag * s, real * s + imag * c
    mag_hi, mag_lo = split(jnp.sqrt(real * real + imag * imag + 1e-12))
    inverse = 1.0 / bin_ref[1:2, :].astype(F32)
    smooth = (mm(mag_hi, band_ref[...]) + mm(mag_lo, band_ref[...])) * inverse + EPS
    return (real / smooth * alive).astype(BF), (imag / smooth * alive).astype(BF)


def flip_matrix(size, channels):
    row = lax.broadcasted_iota(jnp.int32, (size, size), 0)
    col = lax.broadcasted_iota(jnp.int32, (size, size), 1)
    within = lax.rem(row, channels)
    return (col == row - within + (channels - 1 - within)).astype(F32).astype(BF)


def align_kernel(scale, total, out_ref, staged, stored):
    lags, channels, _ = out_ref.shape
    size = GROUP * channels
    flip = flip_matrix(size, channels)
    far = 8 * channels

    def store(g):
        at = pl.ds(g * GROUP, GROUP)
        return pltpu.make_async_copy(staged.at[at], out_ref.at[at], stored.at[g])

    turned = []
    for g in range(lags // GROUP):
        values = (total[:, g * size:(g + 1) * size] * scale).astype(BF)
        values = jnp.concatenate(
            [values[:far], jnp.zeros((128 - channels, size), BF), values[far:]], axis=0)
        turned.append(lax.dot_general(flip, values, (((1,), (1,)), ((), ())), preferred_element_type=F32))
    for g in range(lags // GROUP):
        pieces = []
        for t in range(GROUP):
            piece = pltpu.roll(turned[g][t * channels:(t + 1) * channels, :], 0, 1, stride=1, stride_axis=0)
            pieces.append(piece[:, :NPART].astype(BF))
        result = mm(flip, jnp.concatenate(pieces, axis=0)).astype(BF)
        for t in range(GROUP):
            staged[g * GROUP + t] = result[t * channels:(t + 1) * channels, :]
        store(g).start()
    for g in range(lags // GROUP):
        store(g).wait()


def whole_kernel(devices, windows, records, dead_ref, off_ref, *refs):
    sources, total, refs = refs[:10], refs[10], refs[11:]
    feats, rot, send, recv, held, loaded, mags, norm, cosw, turn, *folded = refs[:18]
    tables, fetched = refs[18:28], refs[28]
    box_ref, taper_ref, te_hi, te_lo, to_hi, to_lo, tw_ref, band_ref, bin_ref, lag_ref = tables
    channels, samples = records.shape
    lags = lag_ref.shape[1]
    half = lags // 2
    i = lax.axis_index("chan")
    r = lax.rem(i, 4)
    x, c = r // 2, lax.rem(r, 2)
    has_prev, has_next, has_third = i >= 4, i + 4 < devices, i + 8 < devices
    prev, following = i - 4, i + 4
    across, partner = i + 2 - 4 * x, i + 1 - 2 * c

    def load(w):
        first = max(0, w * HOP - H)
        last = (w + 1) * HOP - H if w < windows - 1 else samples
        return pltpu.make_async_copy(
            records.at[:, pl.ds(first, last - first)], held.at[:, pl.ds(first + H, last - first)], loaded.at[w])

    def fetch(t):
        return pltpu.make_async_copy(sources[t], tables[t], fetched.at[t])

    first_tables, later_tables = (1, 8, 0), (2, 3, 4, 5, 6, 7, 9)

    barrier = pltpu.get_barrier_semaphore()

    def greet(device):
        pl.semaphore_signal(barrier, inc=1, device_id={"chan": device}, device_id_type=MESH)

    greet(across)
    greet(partner)
    pl.when(has_prev)(lambda: greet(prev))
    pl.when(has_next)(lambda: greet(following))
    slant_out, slant_in = (x == 0) & has_prev, (x == 1) & has_next
    pl.when(slant_out)(lambda: greet(i - 2))
    pl.when(slant_in)(lambda: greet(i + 2))
    late = max(0, windows - 2)

    load(windows - 1).start()
    for t in first_tables:
        fetch(t).start()
    load(windows - 2).start()
    for t in later_tables:
        fetch(t).start()
    for w in reversed(range(windows - 2)):
        load(w).start()

    def all_here():
        others = sum(flag.astype(jnp.int32) for flag in (has_prev, has_next, slant_out, slant_in))
        pl.semaphore_wait(barrier, 2 + others)

    def copy(item, k, source, slot, device):
        return pltpu.make_async_remote_copy(
            src_ref=feats.at[source, k],
            dst_ref=feats.at[slot, k],
            send_sem=send.at[item, k],
            recv_sem=recv.at[slot, k],
            device_id={"chan": device},
            device_id_type=MESH,
        )

    def arrived(slot, k):
        pltpu.make_async_copy(feats.at[slot, k], feats.at[slot, k], recv.at[slot, k]).wait()

    def left(item, k):
        pltpu.make_async_copy(feats.at[0, k], feats.at[0, k], send.at[item, k]).wait()

    def send_own(k):
        pl.when(has_prev)(lambda: copy(0, k, 0, 4, prev).start())
        pl.when(x == 1)(lambda: copy(2, k, 0, 2, across).start())
        pl.when(c == 1)(lambda: copy(4, k, 0, 1, partner).start())

    def forward_next(k, here):
        @pl.when(here & has_next)
        def _():
            arrived(4, k)
            pl.when(has_prev)(lambda: copy(1, k, 4, 8, prev).start())
            pl.when(slant_out & (k >= late))(lambda: copy(8, k, 4, 6, i - 2).start())
            copy(2 + x, k, 4, 2 + 4 * x, across).start()
            copy(4 + c, k, 4, 3 + 2 * c, partner).start()

    def relay_near(k, here):
        @pl.when(here & (i + 2 < devices))
        def _():
            arrived(2, k)
            copy(6, k, 2, 1 + 2 * c, partner).start()

    def forward_third(k, here):
        @pl.when(here & has_third)
        def _():
            arrived(8, k)
            pl.when((x == 0) & (k < late))(lambda: copy(3, k, 8, 6, across).start())
            pl.when(c == 0)(lambda: copy(5, k, 8, 7, partner).start())

    def relay_far(k, here):
        @pl.when(here & (i + 6 < devices))
        def _():
            arrived(6, k)
            copy(7, k, 6, 5 + 2 * c, partner).start()

    def there(k):
        return (k >= 0) & (k < windows)

    def mid_tick(n):
        k = n - FIRST
        forward_next(k, there(k))
        relay_near(k, there(k) & (x == 0))
        k = n - THIRD
        relay_far(k, there(k) & (k < late) & (x == 1))

    def end_tick(n):
        k = n - SECOND
        forward_third(k, there(k))
        relay_near(k, there(k) & (x == 1))
        relay_far(k, there(k) & ((x == 0) | (k >= late)))

    for slot in range(1, 9):
        @pl.when(i + slot >= devices)
        def _(slot=slot):
            feats[slot] = jnp.zeros(feats.shape[1:], BF)

    def rotate(k):
        real, imag = feats[0, k, :, :NF].astype(F32), feats[0, k, :, NF:].astype(F32)

        def put(t, a, b):
            rot[k, t * channels:(t + 1) * channels, :NF] = a.astype(BF)
            rot[k, t * channels:(t + 1) * channels, NF:] = b.astype(BF)

        put(half, real, imag)
        for step in range(1, half + 1):
            t = half - step
            co, si = lag_ref[0, t:t + 1, :], lag_ref[1, t:t + 1, :]
            rc, rs, ic, js = real * co, real * si, imag * co, imag * si
            put(t, rc - js, rs + ic)
            if half + step < lags:
                put(half + step, rc + js, ic - rs)

    def side(ref, units):
        return jnp.concatenate([ref(k) for k in units], axis=1)

    def product(units):
        return lax.dot_general(
            side(lambda k: jnp.concatenate([feats[1:9, k].reshape(8 * channels, 2 * NF), feats[0, k]], axis=0), units),
            side(lambda k: rot[k], units), (((1,), (1,)), ((), ())), preferred_element_type=F32)

    def multiply(units):
        for k in units:
            for slot in (1, 3, 5, 7):
                pl.when(i + slot < devices)(lambda slot=slot, k=k: arrived(slot, k))
        products = product(units)
        if units[0] == 0:
            total[...] = products
        else:
            total[...] += products

    channel = lax.broadcasted_iota(jnp.int32, (channels, 1), 0)
    dead = jnp.zeros((channels, 1), jnp.int32)
    for j in range(channels):
        dead = jnp.where(channel == j, dead_ref[j], dead)
    alive = (1 - dead).astype(F32)
    fetch(1).wait()
    fetch(8).wait()
    prepare_windows(windows, off_ref, taper_ref, bin_ref, cosw, turn)
    held[:, :H] = jnp.zeros((channels, H), F32)
    held[:, samples + H:] = jnp.zeros((channels, H), F32)
    tail = samples // BLK * channels
    norm[tail:, :] = jnp.zeros((norm.shape[0] - tail, BLK), F32)
    fetch(0).wait()
    load(windows - 1).wait()
    mags[:, samples:] = jnp.abs(held[:, samples:]).astype(BF)

    def await_load(w):
        pl.when(w == 0)(lambda: load(0).wait())
        if windows > 2:
            pl.when(w > 0)(lambda: pltpu.make_async_copy(
                records.at[:, pl.ds(H, HOP)], held.at[:, pl.ds(H, HOP)], loaded.at[w]).wait())

    normalise_window(windows - 1, box_ref, held, mags, norm)
    fold_window(windows - 1, off_ref, norm, cosw, *folded[:4])
    load(windows - 2).wait()
    normalise_window(windows - 2, box_ref, held, mags, norm)

    def produce(n, now, later):
        w = windows - 1 - n
        pl.when(w > 1)(lambda: await_load(w - 2))
        mid_tick(n)
        parts = [transform(now[:2], te_hi, te_lo, tw_ref, 0)]
        fold_window(jnp.maximum(w - 1, 0), off_ref, norm, cosw, *later)
        parts.append(transform(now[2:], to_hi, to_lo, tw_ref, 1))
        normalise_window(jnp.maximum(w - 2, 0), box_ref, held, mags, norm)
        rotate(jnp.maximum(n - 1, 0))
        real, imag = whiten(w, parts, alive, band_ref, bin_ref, turn)
        feats[0, n, :, :NF] = real
        feats[0, n, :, NF:] = imag
        send_own(n)
        end_tick(n)

    for t in later_tables:
        fetch(t).wait()
    all_here()

    @pl.loop(0, windows // 2)
    def _(m):
        produce(2 * m, folded[:4], folded[4:])
        produce(2 * m + 1, folded[4:], folded[:4])

    rotate(windows - 1)
    pairs = [range(k, k + 2) for k in range(0, windows, 2)]
    early = [[k for pair in pairs[:-2] for k in pair], range(windows - 4, windows - 1)]
    def hook_of(units):
        return max([2 * (k + SECOND) + 1 for k in units] + [2 * (k + THIRD) for k in units if k < late])

    tasks = []
    tasks += [(hook_of(units), lambda u=units: multiply(u)) for units in early]
    for hook in range(2 * windows, 2 * max(windows + SECOND, late + THIRD)):
        (end_tick if hook % 2 else mid_tick)(hook // 2)
        if tasks and tasks[0][0] <= hook:
            tasks.pop(0)[1]()
    for _, task in tasks:
        task()
    @pl.loop(0, windows)
    def _(k):
        pl.when(has_prev)(lambda: left(0, k))
        pl.when(has_prev & has_next)(lambda: left(1, k))
        pl.when((i + 4 - 4 * x < devices))(lambda: left(2, k))
        pl.when(jnp.where(x == 1, has_next, has_third & (k < late)))(lambda: left(3, k))
        for item, source in ((4, 4 - 4 * c), (5, 8 - 4 * c), (6, 2), (7, 6)):
            pl.when(i + source < devices)(lambda item=item: left(item, k))
        pl.when(slant_out & has_next & (k >= late))(lambda: left(8, k))

    multiply(pairs[-1][1:])


def whole(records, dead_mask, offsets, lags, devices):
    channels, samples = records.shape
    windows = samples // HOP
    count = lags.shape[1]
    consts = spectra_consts() + [lags]
    anywhere = pl.BlockSpec(memory_space=pl.ANY)
    vmem, smem = pl.BlockSpec(memory_space=pltpu.VMEM), pl.BlockSpec(memory_space=pltpu.SMEM)
    rows = NSUB * channels
    total = pl.pallas_call(
        functools.partial(whole_kernel, devices, windows),
        out_shape=pltpu.VMEM((9 * channels, count * channels), F32),
        in_specs=[anywhere, smem, smem] + [anywhere] * len(consts),
        out_specs=vmem,
        scratch_shapes=[
            pltpu.VMEM((9, windows, channels, 2 * NF), BF),
            pltpu.VMEM((windows, count * channels, 2 * NF), BF),
            pltpu.SemaphoreType.DMA((9, windows)),
            pltpu.SemaphoreType.DMA((9, windows)),
            pltpu.VMEM((channels, samples + 2 * H), F32),
            pltpu.SemaphoreType.DMA((windows,)),
            pltpu.VMEM((channels, samples + 2 * H), BF),
            pltpu.VMEM(((samples + HOP + JIT) // BLK * channels, BLK), F32),
            pltpu.VMEM((8 * windows, HALF), F32),
            pltpu.VMEM((2, 8 * windows, NF), F32),
        ] + [pltpu.VMEM((rows, SUB), BF)] * 8
        + [pltpu.VMEM(table.shape, table.dtype) for table in consts]
        + [pltpu.SemaphoreType.DMA((len(consts),))],
        compiler_params=pltpu.CompilerParams(
            collective_id=0, has_side_effects=True, vmem_limit_bytes=56 << 20),
        name="correlate",
    )(records, dead_mask, offsets, *consts)
    return pl.pallas_call(
        functools.partial(align_kernel, 1.0 / math.sqrt(2.0 * NF * windows)),
        out_shape=jax.ShapeDtypeStruct((count, channels, NPART), BF),
        in_specs=[vmem],
        out_specs=pl.BlockSpec(memory_space=pl.ANY),
        scratch_shapes=[
            pltpu.VMEM((count, channels, NPART), BF),
            pltpu.SemaphoreType.DMA((count // GROUP,)),
        ],
        compiler_params=pltpu.CompilerParams(vmem_limit_bytes=8 << 20),
        name="align",
    )(total)


def shifted(value, axis, steps):
    count = lax.axis_size(axis)
    leading, last = (max(0, -steps), min(count, count - steps))
    return lax.ppermute(value, axis, [(source, source + steps) for source in range(leading, last)])


def local(records, dead_mask, offsets):
    channels, samples = records.shape
    tm_count = lax.axis_size("tm")
    tm_index = lax.axis_index("tm")
    windows = samples // HOP
    lags = jnp.asarray(lag_table())
    devices = lax.axis_size("chan")
    if tm_count == 1:
        return whole(records, dead_mask, offsets, lags, devices)
    left = shifted(records[:, -H:], "tm", 1)
    right = shifted(records[:, :HOP + JIT + H], "tm", -1)
    values = jnp.concatenate([left, records, right], axis=1)
    own_offsets = lax.dynamic_slice_in_dim(offsets, tm_index * windows, windows, 0)
    own = spectra(values, dead_mask, own_offsets, True, samples, windows)
    own = lax.all_gather(own, "tm", axis=0, tiled=True)
    lags_local = NLAG // tm_count
    lags = lax.dynamic_slice_in_dim(lags, tm_index * lags_local, lags_local, 1)
    return correlate(own, lags, devices)


def solution(mesh):
    return jax.shard_map(
        local,
        mesh=mesh,
        in_specs=(P(("win", "chan"), "tm"), P(("win", "chan")), P("win")),
        out_specs=P("tm", ("win", "chan"), None),
        check_vma=False,
    )
```
